32 devices in a mesh: blk: 16 (over z, y, core), rep: 2 (over x).
Axes of the slice: x: 2, y: 2, z: 4, core: 2. Of those that a mesh axis runs over, the one named last changes fastest.
Arguments:
- features: bfloat16 [16384, 256], P('blk'), may hold values from -6 to 6
- weight_self: bfloat16 [256, 256], replicated, may hold values from -0.375 to 0.375
- weight_neighbor: bfloat16 [256, 256], replicated, may hold values from -0.375 to 0.375
- bias_vector: float32 [256], replicated, may hold values from -3 to 3
- tile_row: int32 [16, 16, 64], P('blk', 'rep'), may hold values from 0 to 7
- tile_column: int32 [16, 16, 64], P('blk', 'rep'), may hold values from 0 to 7
- tile_value: int32 [16, 16, 64], P('blk', 'rep'), may hold values from 0 to 127
- tile_count: int32 [16, 16], P('blk', 'rep'), may hold values from 16 to 64
- tile_table: bfloat16 [4096, 128, 128], P(('blk', 'rep')), may hold values from -0.0625 to 0.0625
- cotangent: bfloat16 [16384, 256], P('blk'), may hold values from -6 to 6
Outputs:
- activations: bfloat16 [16384, 256], P('blk')
- grad_features: bfloat16 [16384, 256], P('blk')
- grad_weight_self: float32 [256, 256], replicated
- grad_weight_neighbor: float32 [256, 256], replicated
- grad_bias: float32 [256], replicated
The draws below stay inside these ranges and needn't reach their ends.
All inputs are finite; a program needn't handle non-finite values.
Results may differ from the reference program's by a relative error of at most 0.025.
Values may be sent and summed in bfloat16 or wider, within the bound.
A program may use at most 64 MiB of HBM per device.

```python
import jax
import jax.numpy as jnp
from jax import lax

F = 256
TILE = 128
R_DEV = 1024
SLOTS = 64
VALS = 128
BLOCKS_DEV = 8
GROUPS = 16
STEPS = 16
NODES = 16384
TABLE_TILES = 4096
N_BLK = 16
N_REP = 2


def draw_tile_count(key, part):
    step_ids = jnp.arange(STEPS, dtype=jnp.int32)
    distance = jnp.minimum(step_ids, STEPS - step_ids)
    drawn = jax.random.randint(key, (GROUPS, STEPS), SLOTS // 4, SLOTS // 2 + 1, dtype=jnp.int32)
    return jnp.where(distance[None, :] <= 1, SLOTS, drawn).astype(jnp.int32)


def touch_ends(entries, key, low, top_value):
    extent = entries.shape
    place = [jax.random.randint(jax.random.fold_in(key, axis), (), 0, extent[axis]) for axis in range(len(extent))]
    entries = entries.at[tuple(place)].set(low)
    longest = extent.index(max(extent))
    place[longest] = (place[longest] + 1) % extent[longest]
    return entries.at[tuple(place)].set(top_value)


def steps_of(rng, extent, split, smallest, high):
    gain = 1.0
    for dim, blocks in split:
        draws = jax.random.uniform(jax.random.fold_in(jax.random.fold_in(rng, 6), dim), (blocks,), jnp.float32, smallest / len(split), high / len(split))
        gain = gain * jnp.repeat(jnp.exp(draws), extent[dim] // blocks).reshape((-1,) + (1,) * (len(extent) - 1 - dim))
    return gain


def scatter_about(own_key, extent, width, bound, pieces=(), kind=jnp.bfloat16):
    gain = steps_of(own_key, extent, pieces, -0.22, 0.18) if pieces else 1.0
    result = jax.random.normal(own_key, extent, jnp.float32) * width * gain
    return jnp.minimum(jnp.maximum(result, -bound), bound).astype(kind)


def setup_inputs(seed: int = 0) -> dict:
    streams_of = jax.random.split(jax.random.key(seed), 11)
    features = scatter_about(streams_of[0], (NODES, F), 1.0, 6.0, ((0, 16),))
    weight_self = scatter_about(streams_of[1], (F, F), F ** -0.5, 0.375)
    weight_neighbor = scatter_about(streams_of[2], (F, F), F ** -0.5, 0.375)
    bias_vector = scatter_about(streams_of[3], (F,), 0.5, 3.0, (), jnp.float32)
    tile_row = touch_ends(jax.random.randint(streams_of[4], (GROUPS, STEPS, SLOTS), 0, BLOCKS_DEV), jax.random.fold_in(streams_of[4], 1), 0, BLOCKS_DEV - 1).astype(jnp.int32)
    tile_column = touch_ends(jax.random.randint(streams_of[5], (GROUPS, STEPS, SLOTS), 0, BLOCKS_DEV), jax.random.fold_in(streams_of[5], 1), 0, BLOCKS_DEV - 1).astype(jnp.int32)
    tile_value = touch_ends(jax.random.randint(streams_of[6], (GROUPS, STEPS, SLOTS), 0, VALS), jax.random.fold_in(streams_of[6], 1), 0, VALS - 1).astype(jnp.int32)
    tile_count = draw_tile_count(jax.random.fold_in(streams_of[10], 71), 0)
    tile_table = scatter_about(streams_of[8], (TABLE_TILES, TILE, TILE), (TILE * SLOTS * STEPS * TILE // (2 * R_DEV)) ** -0.5, 0.0625, ((0, 32),))
    cotangent = scatter_about(streams_of[9], (NODES, F), 1.0, 6.0, ((0, 16),))
    return dict(features=features, weight_self=weight_self, weight_neighbor=weight_neighbor, bias_vector=bias_vector, tile_row=tile_row, tile_column=tile_column, tile_value=tile_value, tile_count=tile_count, tile_table=tile_table, cotangent=cotangent)


def reference(features, weight_self, weight_neighbor, bias_vector, tile_row, tile_column, tile_value, tile_count, tile_table, cotangent):
    block_count = R_DEV // TILE
    step_count = N_BLK // N_REP
    step_ids = jnp.arange(N_BLK, dtype=jnp.int32)
    slot_index = jnp.arange(SLOTS, dtype=jnp.int32)
    block_index = jnp.arange(block_count, dtype=jnp.int32)
    value_table = tile_table.astype(jnp.float32)
    source_blocks = features.astype(jnp.float32).reshape(N_BLK, block_count, TILE, F)

    def lists_of(group_id):
        table_base = (group_id * N_REP + step_ids // step_count) * VALS
        tile_values = value_table[table_base[:, None] + tile_value[group_id]]
        is_live = slot_index[None, :] < tile_count[group_id][:, None]
        rows_hit = ((tile_row[group_id][..., None] == block_index) & is_live[..., None]).astype(jnp.float32)
        columns_hit = ((tile_column[group_id][..., None] == block_index) & is_live[..., None]).astype(jnp.float32)
        partner = ((group_id - step_ids) % N_BLK).astype(jnp.int32)
        return tile_values, rows_hit, columns_hit, partner

    def forward_group(group_id):
        tile_values, rows_hit, columns_hit, partner = lists_of(group_id)
        picked = source_blocks[partner[:, None], tile_column[group_id]]
        products = jnp.einsum("skab,skbf->skaf", tile_values, picked)
        return jnp.einsum("skr,skaf->raf", rows_hit, products)

    aggregate = lax.map(forward_group, step_ids)
    aggregate_b = aggregate.reshape(NODES, F).astype(jnp.bfloat16)
    before = jnp.dot(features, weight_self, preferred_element_type=jnp.float32)
    before = before + jnp.dot(aggregate_b, weight_neighbor, preferred_element_type=jnp.float32) + bias_vector
    sigmoid_pre = jax.nn.sigmoid(before)
    activations = (before * sigmoid_pre).astype(jnp.bfloat16)
    derivative = sigmoid_pre * (1.0 + before * (1.0 - sigmoid_pre))
    grad_pre = (cotangent.astype(jnp.float32) * derivative).astype(jnp.bfloat16)
    grad_weight_self = jnp.dot(features.T, grad_pre, preferred_element_type=jnp.float32)
    grad_weight_neighbor = jnp.dot(aggregate_b.T, grad_pre, preferred_element_type=jnp.float32)
    grad_bias = jnp.sum(grad_pre.astype(jnp.float32), axis=0)
    self_term = jnp.dot(grad_pre, weight_self.T, preferred_element_type=jnp.float32)
    sent_back = jnp.dot(grad_pre, weight_neighbor.T, preferred_element_type=jnp.float32).astype(jnp.bfloat16)
    sent_blocks = sent_back.astype(jnp.float32).reshape(N_BLK, block_count, TILE, F)

    def backward_group(running, group_id):
        tile_values, rows_hit, columns_hit, partner = lists_of(group_id)
        picked = sent_blocks[group_id][tile_row[group_id]]
        products = jnp.einsum("skab,skaf->skbf", tile_values, picked)
        addition = jnp.einsum("skc,skbf->scbf", columns_hit, products)
        return running.at[partner].add(addition), None

    pushed, unused = lax.scan(backward_group, jnp.zeros((N_BLK, block_count, TILE, F), jnp.float32), step_ids)
    grad_features = (self_term + pushed.reshape(NODES, F)).astype(jnp.bfloat16)
    return activations, grad_features, grad_weight_self, grad_weight_neighbor, grad_bias
```

```python
import functools

import jax
import jax.numpy as jnp
from jax import lax
from jax.experimental import pallas as pl
from jax.experimental.pallas import tpu as pltpu
from jax.sharding import PartitionSpec as P

ROWS_ROWS = (((0,), (0,)), ((), ()))
COLS_COLS = (((1,), (1,)), ((), ()))


def build_kernel(rows, columns, values, counts, table, dense):
    step = pl.program_id(0)
    tile = table.shape[1]
    dense[...] = jnp.zeros_like(dense)

    def add_tile(slot, carry):
        row = pl.multiple_of(rows[step, slot] * tile, tile)
        column = pl.multiple_of(columns[step, slot] * tile, tile)
        place = (0, pl.ds(row, tile), pl.ds(column, tile))
        dense[place] = dense[place] + table[values[step, slot]]
        return carry

    lax.fori_loop(0, counts[step], add_tile, 0)


def build_dense(rows, columns, values, counts, table, row_total):
    step_count = rows.shape[0]
    return pl.pallas_call(
        build_kernel,
        grid_spec=pltpu.PrefetchScalarGridSpec(
            num_scalar_prefetch=4,
            grid=(step_count,),
            in_specs=[pl.BlockSpec(table.shape, lambda s, *_: (0, 0, 0))],
            out_specs=pl.BlockSpec((1, row_total, row_total), lambda s, *_: (s, 0, 0)),
        ),
        out_shape=jax.ShapeDtypeStruct((step_count, row_total, row_total), jnp.bfloat16),
        cost_estimate=pl.CostEstimate(
            flops=0, bytes_accessed=20 * 2**20, transcendentals=0
        ),
        name="build",
    )(rows, columns, values, counts, table)


def ring_place(cycle, replicas):
    group = lax.axis_index("blk")
    replica = lax.axis_index("rep")
    reverse = (2 * replica) // replicas if replicas > 1 else 0 * replica
    ahead = lax.rem(group + 1 - 2 * reverse + cycle, cycle)
    behind = lax.rem(group - 1 + 2 * reverse + cycle, cycle)
    return group, replica, reverse, ahead, behind


def greet(devices):
    barrier = pltpu.get_barrier_semaphore()
    for device in devices:
        pl.semaphore_signal(
            barrier, inc=1, device_id={"blk": device},
            device_id_type=pl.DeviceIdType.MESH,
        )
    pl.semaphore_wait(barrier, len(devices))


def forward_kernel(
    cycle, replicas, pieces, features, dense, out,
    slots, blocks, total, block_sem, first_sem, send_sem, recv_sem,
):
    steps, rows = blocks.shape[0], blocks.shape[1]
    _, _, reverse, ahead, behind = ring_place(cycle, replicas)
    size = rows // pieces
    first = pltpu.make_async_copy(features, slots.at[0], first_sem)
    first.start()

    def load(step):
        return pltpu.make_async_copy(
            dense.at[step], blocks.at[step], block_sem.at[step]
        )

    def in_order(hop):
        return hop * (1 - reverse) + (steps - hop) * reverse

    @pl.loop(0, steps)
    def _(hop):
        load(in_order(hop + reverse)).start()

    greet((ahead, behind))
    first.wait()

    def hop_copy(hop, piece):
        span = pl.ds(piece * size, size)
        return pltpu.make_async_remote_copy(
            src_ref=slots.at[hop, span],
            dst_ref=slots.at[hop + 1, span],
            send_sem=send_sem.at[hop, piece],
            recv_sem=recv_sem.at[hop, piece],
            device_id={"blk": ahead},
            device_id_type=pl.DeviceIdType.MESH,
        )

    total[...] = jnp.zeros_like(total)
    hops = steps - 1 + reverse

    @pl.loop(0, hops + 1)
    def _(hop):
        for piece in range(pieces):
            @pl.when(hop > 0)
            def _():
                hop_copy(hop - 1, piece).wait_recv()

            @pl.when(hop < hops)
            def _():
                hop_copy(hop, piece).start()

        step = in_order(hop)

        @pl.when(step < steps)
        def _():
            load(step).wait()
            total[...] += jnp.dot(
                blocks[step], slots[hop], preferred_element_type=jnp.float32
            )

    out[...] = total[...].astype(out.dtype)

    @pl.loop(0, hops)
    def _(hop):
        for piece in range(pieces):
            hop_copy(hop, piece).wait_send()


LANES = 4


def is_layered(cycle, replicas):
    return (
        cycle // replicas == 2 * LANES and cycle >= 3 * LANES
        and cycle % LANES == 0 and replicas == 2
    )


def forward(cycle, replicas, features, dense):
    step_count, row_total, _ = dense.shape
    width = features.shape[1]
    pieces = 4
    slots, sems = (step_count + 1, row_total, width), (step_count, pieces)
    return pl.pallas_call(
        functools.partial(forward_kernel, cycle, replicas, pieces),
        in_specs=[pl.BlockSpec(memory_space=pl.ANY)] * 2,
        out_specs=pl.BlockSpec(memory_space=pltpu.VMEM),
        out_shape=jax.ShapeDtypeStruct((row_total, width), jnp.bfloat16),
        scratch_shapes=[
            pltpu.VMEM(slots, jnp.bfloat16),
            pltpu.VMEM(dense.shape, jnp.bfloat16),
            pltpu.VMEM((row_total, width), jnp.float32),
            pltpu.SemaphoreType.DMA((step_count,)),
            pltpu.SemaphoreType.DMA,
            pltpu.SemaphoreType.DMA(sems),
            pltpu.SemaphoreType.DMA(sems),
        ],
        compiler_params=pltpu.CompilerParams(collective_id=0, has_side_effects=True),
        name="forward",
    )(features, dense)


def layer_kernel(
    features, mine, other, weight_self, weight_neighbor, bias, cotangent,
    activations, sent_t, self_t, grads,
):
    f32 = jnp.float32
    width = features.shape[1]
    aggregate = (mine[...].astype(f32) + other[...].astype(f32)).astype(jnp.bfloat16)
    pre = (
        jnp.dot(features[...], weight_self[...], preferred_element_type=f32)
        + jnp.dot(aggregate, weight_neighbor[...], preferred_element_type=f32)
        + bias[...]
    )
    sigmoid = jax.nn.sigmoid(pre)
    activations[...] = (pre * sigmoid).astype(activations.dtype)
    derivative = sigmoid * (1.0 + pre * (1.0 - sigmoid))
    grad_pre = (cotangent[...].astype(f32) * derivative).astype(jnp.bfloat16)
    sent_t[...] = lax.dot_general(
        weight_neighbor[...], grad_pre, COLS_COLS, preferred_element_type=f32
    ).astype(sent_t.dtype)
    self_t[...] = lax.dot_general(
        weight_self[...], grad_pre, COLS_COLS, preferred_element_type=f32
    )
    grad_self = lax.dot_general(
        features[...], grad_pre, ROWS_ROWS, preferred_element_type=f32
    ).astype(grads.dtype)
    grad_neighbor = lax.dot_general(
        aggregate, grad_pre, ROWS_ROWS, preferred_element_type=f32
    ).astype(grads.dtype)
    summed = jnp.sum(grad_pre.astype(f32), axis=0, keepdims=True)
    parts = grads.shape[0]
    depth = 2 * width // parts
    tail = grads.shape[1] - depth
    bias_rows = jnp.broadcast_to(summed, (tail, width)).astype(grads.dtype)
    for part in range(parts):
        source, place = (
            (grad_self, part) if 2 * part < parts else (grad_neighbor, part - parts // 2)
        )
        grads[part, 0:depth, :] = source[place * depth : (place + 1) * depth, :]
        grads[part, depth:, :] = bias_rows


def layer(parts, features, mine, other, weight_self, weight_neighbor, bias, cotangent):
    row_total, width = features.shape
    shape = jax.ShapeDtypeStruct
    return pl.pallas_call(
        layer_kernel,
        out_shape=(
            shape((row_total, width), jnp.bfloat16),
            shape((width, row_total), jnp.bfloat16),
            shape((width, row_total), jnp.float32),
            shape((parts, 2 * width // parts + 16, width), jnp.bfloat16),
        ),
        name="layer",
    )(features, mine, other, weight_self, weight_neighbor, bias, cotangent)


def backward_kernel(
    cycle, replicas, pieces, sent_t, dense, grads, out, part_out,
    landed, held, part_landed, part_held, blocks, term,
    block_sem, send_sem, recv_sem,
):
    steps = blocks.shape[0]
    width = sent_t.shape[0]
    size = width // pieces
    f32 = jnp.float32
    group, replica, reverse, behind, ahead = ring_place(cycle, replicas)

    def load(step):
        return pltpu.make_async_copy(
            dense.at[step], blocks.at[step], block_sem.at[step]
        )

    def in_order(hop):
        return (steps - 1 - hop) * (1 - reverse) + hop * reverse

    @pl.loop(0, steps)
    def _(hop):
        load(in_order(hop)).start()

    greet((ahead, behind))

    def hop_copy(hop, piece):
        if piece < pieces:
            span = pl.ds(piece * size, size)
            source, target = held.at[hop, span], landed.at[hop, span]
        else:
            source, target = part_held.at[hop], part_landed.at[hop]
        return pltpu.make_async_remote_copy(
            src_ref=source,
            dst_ref=target,
            send_sem=send_sem.at[hop, piece],
            recv_sem=recv_sem.at[hop, piece],
            device_id={"blk": ahead},
            device_id_type=pl.DeviceIdType.MESH,
        )

    hops = steps - 1 + reverse

    @pl.loop(0, steps)
    def _(hop):
        step = in_order(hop)
        target = lax.rem(group - steps * replica - step + 2 * cycle, cycle)
        load(step).wait()
        term[...] = jnp.dot(sent_t[...], blocks[step], preferred_element_type=f32)
        for piece in range(pieces + 1):
            span = pl.ds(piece * size, size)

            @pl.when(hop > 0)
            def _():
                hop_copy(hop - 1, piece).wait_recv()
                if piece < pieces:
                    held[hop, span] = (
                        term[span] + landed[hop - 1, span].astype(f32)
                    ).astype(held.dtype)
                else:
                    part_held[hop] = (
                        grads[target].astype(f32) + part_landed[hop - 1].astype(f32)
                    ).astype(part_held.dtype)

            @pl.when(hop == 0)
            def _():
                if piece < pieces:
                    held[hop, span] = term[span].astype(held.dtype)
                else:
                    part_held[hop] = grads[target]

            @pl.when(hop < hops)
            def _():
                hop_copy(hop, piece).start()

    @pl.when(reverse == 0)
    def _():
        out[...] = held[steps - 1]
        part_out[...] = part_held[steps - 1]

    @pl.when(reverse == 1)
    def _():
        for piece in range(pieces + 1):
            hop_copy(steps - 1, piece).wait_recv()
        out[...] = landed[steps - 1]
        part_out[...] = part_landed[steps - 1]

    @pl.loop(0, hops)
    def _(hop):
        for piece in range(pieces + 1):
            hop_copy(hop, piece).wait_send()


def backward(cycle, replicas, sent_t, dense, grads):
    step_count, row_total, _ = dense.shape
    width = sent_t.shape[0]
    part = grads.shape[1:]
    pieces = 4
    bf16 = jnp.bfloat16
    return pl.pallas_call(
        functools.partial(backward_kernel, cycle, replicas, pieces),
        in_specs=[
            pl.BlockSpec(memory_space=pltpu.VMEM),
            pl.BlockSpec(memory_space=pl.ANY),
            pl.BlockSpec(memory_space=pltpu.VMEM),
        ],
        out_specs=[pl.BlockSpec(memory_space=pltpu.VMEM)] * 2,
        out_shape=(
            jax.ShapeDtypeStruct((width, row_total), bf16),
            jax.ShapeDtypeStruct(part, bf16),
        ),
        scratch_shapes=[
            pltpu.VMEM((step_count, width, row_total), bf16),
            pltpu.VMEM((step_count, width, row_total), bf16),
            pltpu.VMEM((step_count, *part), bf16),
            pltpu.VMEM((step_count, *part), bf16),
            pltpu.VMEM(dense.shape, bf16),
            pltpu.VMEM((width, row_total), jnp.float32),
            pltpu.SemaphoreType.DMA((step_count,)),
            pltpu.SemaphoreType.DMA((step_count, pieces + 1)),
            pltpu.SemaphoreType.DMA((step_count, pieces + 1)),
        ],
        compiler_params=pltpu.CompilerParams(collective_id=1, has_side_effects=True),
        name="backward",
    )(sent_t, dense, grads)


def finish_kernel(
    cycle, replicas, pushed, part, self_t, weights, bias_out, grad_t,
    gathered, landed, part_landed, pair_send, pair_recv, send_sem, recv_sem,
):
    f32 = jnp.float32
    depth = gathered.shape[1]
    group = lax.axis_index("blk")
    partner = {"rep": lax.rem(lax.axis_index("rep") + replicas // 2, replicas)}
    mesh_id = pl.DeviceIdType.MESH
    barrier = pltpu.get_barrier_semaphore()
    pl.semaphore_signal(barrier, inc=1, device_id=partner, device_id_type=mesh_id)
    for away in range(1, cycle):
        pl.semaphore_signal(
            barrier, inc=1, device_id={"blk": lax.rem(group + away, cycle)},
            device_id_type=mesh_id,
        )
    pl.semaphore_wait(barrier, cycle)

    def swap(source, target, index):
        return pltpu.make_async_remote_copy(
            src_ref=source, dst_ref=target,
            send_sem=pair_send.at[index], recv_sem=pair_recv.at[index],
            device_id=partner, device_id_type=mesh_id,
        )

    part_swap = swap(part, part_landed, 0)
    part_swap.start()
    panel_swap = swap(pushed, landed, 1)
    panel_swap.start()
    part_swap.wait()
    summed = part[...].astype(f32) + part_landed[...].astype(f32)
    bias_out[...] = summed[depth:]
    gathered[group] = summed[:depth].astype(gathered.dtype)

    def put(away):
        return pltpu.make_async_remote_copy(
            src_ref=gathered.at[group],
            dst_ref=gathered.at[group],
            send_sem=send_sem.at[away],
            recv_sem=recv_sem.at[away],
            device_id={"blk": lax.rem(group + away, cycle)},
            device_id_type=mesh_id,
        )

    @pl.loop(1, cycle)
    def _(away):
        put(away).start()

    @pl.loop(1, cycle)
    def _(away):
        put(away).wait()

    weights[...] = gathered[...].astype(f32)
    panel_swap.wait()
    grad_t[...] = (
        self_t[...] + (pushed[...].astype(f32) + landed[...].astype(f32))
    ).astype(grad_t.dtype)


def finish(cycle, replicas, pushed, part, self_t):
    width = pushed.shape[0]
    depth = 2 * width // cycle
    tail = part.shape[0] - depth
    shape = jax.ShapeDtypeStruct
    return pl.pallas_call(
        functools.partial(finish_kernel, cycle, replicas),
        in_specs=[pl.BlockSpec(memory_space=pltpu.VMEM)] * 3,
        out_specs=[pl.BlockSpec(memory_space=pltpu.VMEM)] * 3,
        out_shape=(
            shape((cycle, depth, width), jnp.float32),
            shape((tail, width), jnp.float32),
            shape(pushed.shape, jnp.bfloat16),
        ),
        scratch_shapes=[
            pltpu.VMEM((cycle, depth, width), jnp.bfloat16),
            pltpu.VMEM(pushed.shape, jnp.bfloat16),
            pltpu.VMEM(part.shape, jnp.bfloat16),
            pltpu.SemaphoreType.DMA((2,)),
            pltpu.SemaphoreType.DMA((2,)),
            pltpu.SemaphoreType.DMA((cycle,)),
            pltpu.SemaphoreType.DMA((cycle,)),
        ],
        compiler_params=pltpu.CompilerParams(collective_id=2, has_side_effects=True),
        name="finish",
    )(pushed, part, self_t)


class Spot:
    def __init__(self, cycle, steps):
        self.steps, self.layers = steps, cycle // LANES
        self.group, self.replica = lax.axis_index("blk"), lax.axis_index("rep")
        self.sign = 1 - 2 * self.replica
        self.layer, self.lane = self.group // LANES, lax.rem(self.group, LANES)
        self.pair, self.core = self.lane // 2, lax.rem(self.lane, 2)
        self.lane_across = (1 - self.pair) * 2 + self.core
        self.lane_beside = self.pair * 2 + 1 - self.core
        self.across = self.layer * LANES + self.lane_across
        self.beside = self.layer * LANES + self.lane_beside

    def layer_at(self, distance):
        return lax.rem(self.layer + distance + 2 * self.layers, self.layers)

    def at_layer(self, distance):
        return self.layer_at(distance) * LANES + self.lane

    def step(self, lane, other_lane, distance):
        return (
            self.replica * self.steps + lane - other_lane
            + self.sign * LANES * distance
        )

    def meets(self, lane, other_lane, distance):
        step = self.step(lane, other_lane, distance)
        return jnp.logical_and(step >= 0, step < self.steps)

    def chip_meets(self, pair, other_lane, distance):
        return jnp.logical_or(
            self.meets(2 * pair, other_lane, distance),
            self.meets(2 * pair + 1, other_lane, distance),
        )

    def layer_meets(self, other_lane, distance):
        return jnp.logical_or(
            self.chip_meets(0, other_lane, distance),
            self.chip_meets(1, other_lane, distance),
        )

    def greet(self):
        barrier = pltpu.get_barrier_semaphore()
        signal = functools.partial(
            pl.semaphore_signal, barrier, inc=1, device_id_type=pl.DeviceIdType.MESH
        )
        signal(device_id={"blk": self.across})
        signal(device_id={"blk": self.beside})
        signal(device_id={"rep": 1 - self.replica})
        for away in range(1, self.layers):
            signal(device_id={"blk": self.at_layer(away)})
        pl.semaphore_wait(barrier, 2 + self.layers)


def remote(source, target, sems, index, device):
    send, recv = sems
    return pltpu.make_async_remote_copy(
        src_ref=source, dst_ref=target,
        send_sem=send.at[index], recv_sem=recv.at[index],
        device_id=device, device_id_type=pl.DeviceIdType.MESH,
    )


def layered_backward_kernel(
    cycle, pieces, sent_t, self_t, dense, grads,
    grad_out, weight_self_out, weight_neighbor_out, bias_out,
    blocks, acc, core_out, core_in, pair_out, pair_in, layer_out, layer_in,
    rep_out, rep_in, far_out, far_in, part_acc, core_part, pair_part_out, pair_part,
    layer_part_out, layer_part, rep_part_out, rep_part, gathered, block_sem,
    *sems,
):
    f32 = jnp.float32
    bf16 = jnp.bfloat16
    steps, rows = blocks.shape[0], blocks.shape[1]
    size = rows // pieces
    at = Spot(cycle, steps)
    layers = at.layers
    depth = gathered.shape[2]
    (core_sems, pair_sems, layer_sems, rep_sems, core_part_sems, pair_part_sems,
     layer_part_sems, rep_part_sems, spread_sems, widen_sems, far_sems) = [
        (sems[2 * k], sems[2 * k + 1]) for k in range(11)
    ]
    by_layer = pieces // 2
    partner = {"rep": 1 - at.replica}
    onward = {"blk": at.at_layer(-at.sign)}

    def load(step):
        return pltpu.make_async_copy(
            dense.at[step], blocks.at[step], block_sem.at[step]
        )

    @pl.loop(0, steps)
    def _(hop):
        load((steps - 1 - hop) * (1 - at.replica) + hop * at.replica).start()

    at.greet()

    def own_lane(side):
        return 2 * side + at.core

    def other_lane(side):
        return 2 * side + 1 - at.core

    def span(n):
        return pl.ds(pl.multiple_of(n * size, size), size)

    def core_copy(i, side):
        return remote(core_out.at[i, side], core_in.at[i, side], core_sems, (i, side),
                      {"blk": at.beside})

    def pair_copy(i):
        return remote(pair_out.at[i], pair_in.at[i], pair_sems, i, {"blk": at.across})

    def layer_copy(i):
        return remote(layer_out.at[i], layer_in.at[i], layer_sems, i, onward)

    def far_copy(n):
        return remote(far_out.at[n], far_in.at[n], far_sems, n, onward)

    def rep_copy(n):
        return remote(rep_out.at[n], rep_in.at[n], rep_sems, n, partner)

    def part_of(d, lane):
        return at.layer_at(-at.sign * d) * LANES + lane

    def core_part_copy(d, side):
        return remote(grads.at[part_of(d, other_lane(side))], core_part.at[d, side],
                      core_part_sems, (d, side), {"blk": at.beside})

    def pair_part_copy(d):
        return remote(pair_part_out.at[d], pair_part.at[d], pair_part_sems, d,
                      {"blk": at.across})

    def layer_part_copy(d):
        return remote(layer_part_out.at[d - 1], layer_part.at[d - 1], layer_part_sems,
                      d - 1, onward)

    def rep_part_copy():
        return remote(rep_part_out, rep_part, rep_part_sems, 0, partner)

    def spread(away):
        here = gathered.at[at.lane, at.layer]
        return remote(here, here, spread_sems, away, {"blk": at.at_layer(away)})

    def widen(k):
        lane = at.lane_across if k == 2 else at.lane
        device = at.across if k == 0 else at.beside
        return remote(gathered.at[lane], gathered.at[lane], widen_sems, k,
                      {"blk": device})

    def sends_core(d, side):
        return at.meets(at.lane, other_lane(side), d)

    def gets_core(d, side):
        return at.meets(at.lane_beside, own_lane(side), d)

    def early(d, n):
        return jnp.logical_and(d == 2, n < by_layer)

    def sends_far(n):
        return jnp.logical_and(n < by_layer, at.chip_meets(at.pair, at.lane_across, 2))

    def sends_pair(d, n=None):
        here = at.chip_meets(at.pair, at.lane_across, d)
        if n is None:
            return here
        return jnp.logical_and(here, jnp.logical_not(early(d, n)))

    def gets_pair(d, n=None):
        there = at.chip_meets(1 - at.pair, at.lane, d)
        if n is None:
            return there
        return jnp.logical_and(there, jnp.logical_not(early(d, n)))

    def sends_layer(d, n=None):
        far = at.layer_meets(at.lane, 2)
        if n is not None:
            far = jnp.logical_or(
                at.chip_meets(at.pair, at.lane, 2),
                jnp.logical_and(far, n >= by_layer),
            )
        return jnp.logical_and(d > 0, jnp.logical_or(d == 1, far))

    def gets_layer(d, n):
        return jnp.logical_and(d < 2, sends_layer(d + 1, n))

    def product(i, d, n, lane, store):
        step = at.step(at.lane, lane, d)

        @pl.when(n == 0)
        def _():
            load(step).wait()

        wide = pl.ds(pl.multiple_of(n * size, 2 * size), 2 * size)
        value = jnp.dot(
            sent_t[...], blocks[step, :, wide], preferred_element_type=f32
        )
        store(i, value[:, :size])
        store(i + 1, value[:, size:])

    def begin(i):
        d, n = 2 - i // pieces, lax.rem(i, pieces)
        for side in range(2):
            @pl.when(sends_core(d, side))
            def _():
                def store(i, value):
                    core_out[i, side] = value.astype(bf16)

                product(i, d, n, other_lane(side), store)
                core_copy(i, side).start()
                core_copy(i + 1, side).start()

        for side in range(2):
            own = at.meets(at.lane, own_lane(side), d)

            @pl.when(own)
            def _():
                def store(i, value):
                    acc[i, side] = value

                product(i, d, n, own_lane(side), store)

            @pl.when(jnp.logical_not(own))
            def _():
                for k in range(2):
                    acc[i + k, side] = jnp.zeros(acc.shape[2:], f32)

    def over_pair(i):
        d, n = 2 - i // pieces, lax.rem(i, pieces)
        for side in range(2):
            @pl.when(gets_core(d, side))
            def _():
                core_copy(i, side).wait_recv()
                acc[i, side] += core_in[i, side].astype(f32)

        @pl.when(jnp.logical_and(d == 2, sends_far(n)))
        def _():
            far_out[n] = acc[i, 1 - at.pair].astype(bf16)
            far_copy(n).start()

        @pl.when(jnp.logical_and(d == 1, sends_far(n)))
        def _():
            far_copy(n).wait_recv()
            acc[i, 1 - at.pair] += far_in[n].astype(f32)

        @pl.when(sends_pair(d, n))
        def _():
            pair_out[i] = acc[i, 1 - at.pair].astype(bf16)
            pair_copy(i).start()

    def over_layers(i):
        d, n = 2 - i // pieces, lax.rem(i, pieces)

        @pl.when(gets_pair(d, n))
        def _():
            pair_copy(i).wait_recv()
            acc[i, at.pair] += pair_in[i].astype(f32)

        @pl.when(gets_layer(d, n))
        def _():
            layer_copy(i - pieces).wait_recv()
            acc[i, at.pair] += layer_in[i - pieces].astype(f32)

        @pl.when(sends_layer(d, n))
        def _():
            layer_out[i] = acc[i, at.pair].astype(bf16)
            layer_copy(i).start()

        @pl.when(d == 0)
        def _():
            rep_out[n] = acc[i, at.pair].astype(bf16)
            rep_copy(n).start()

            @pl.when(n > 0)
            def _():
                close(n - 1)

    def parts_to_core():
        for d in range(3):
            for side in range(2):
                pl.when(sends_core(d, side))(
                    lambda: core_part_copy(d, side).start()
                )

    def parts_to_pair():
        for d in range(3):
            for side in range(2):
                own = at.meets(at.lane, own_lane(side), d)
                part_acc[d, side] = grads[part_of(d, own_lane(side))].astype(
                    f32
                ) * own.astype(f32)

                @pl.when(gets_core(d, side))
                def _():
                    core_part_copy(d, side).wait_recv()
                    part_acc[d, side] += core_part[d, side].astype(f32)

            @pl.when(sends_pair(d))
            def _():
                pair_part_out[d] = part_acc[d, 1 - at.pair].astype(bf16)
                pair_part_copy(d).start()

    def part_onward(d):
        @pl.when(gets_pair(d))
        def _():
            pair_part_copy(d).wait_recv()
            part_acc[d, at.pair] += pair_part[d].astype(f32)

        if d < 2:
            @pl.when(sends_layer(d + 1))
            def _():
                layer_part_copy(d + 1).wait_recv()
                part_acc[d, at.pair] += layer_part[d].astype(f32)

        if d > 0:
            @pl.when(sends_layer(d))
            def _():
                layer_part_out[d - 1] = part_acc[d, at.pair].astype(bf16)
                layer_part_copy(d).start()
        else:
            rep_part_out[...] = part_acc[0, at.pair].astype(bf16)
            rep_part_copy().start()

    def part_spread():
        rep_part_copy().wait_recv()
        summed = rep_part_out[...].astype(f32) + rep_part[...].astype(f32)
        bias_out[...] = summed[depth : depth + 1]
        gathered[at.lane, at.layer] = summed[:depth].astype(bf16)
        for away in range(1, layers):
            spread(away).start()

    def part_over_pair():
        for away in range(1, layers):
            spread(away).wait_recv()
        widen(0).start()

    def part_over_core():
        widen(0).wait_recv()
        widen(1).start()
        widen(2).start()

    def close(n):
        rep_copy(n).wait_recv()
        total = (
            self_t[:, span(n)] + rep_out[n].astype(f32) + rep_in[n].astype(f32)
        )
        grad_out[span(n), :] = total.T.astype(grad_out.dtype)

    timetable = (
        (0, parts_to_core),
        (2, parts_to_pair),
        (pieces + 2, functools.partial(part_onward, 2)),
        (2 * pieces + 1, functools.partial(part_onward, 1)),
        (2 * pieces + 3, functools.partial(part_onward, 0)),
        (3 * pieces, part_spread),
        (3 * pieces + 2, part_over_pair),
        (3 * pieces + 3, part_over_core),
    )

    @pl.loop(0, 4 * pieces)
    def _(i):
        @pl.when(jnp.logical_and(i < 3 * pieces, lax.rem(i, 2) == 0))
        def _():
            begin(i)

        @pl.when(jnp.logical_and(i > 0, i <= 3 * pieces))
        def _():
            over_pair(i - 1)

        @pl.when(i >= pieces)
        def _():
            over_layers(i - pieces)

        for turn, act in timetable:
            pl.when(i == turn)(act)

    widen(1).wait_recv()
    widen(2).wait_recv()
    per_weight = cycle // 2
    for layer in range(layers):
        for lane in range(LANES):
            part = layer * LANES + lane
            out = weight_self_out if part < per_weight else weight_neighbor_out
            place = part % per_weight * depth
            out[place : place + depth, :] = gathered[lane, layer].astype(f32)
    close(pieces - 1)

    @pl.loop(0, 3 * pieces)
    def _(i):
        d, n = 2 - i // pieces, lax.rem(i, pieces)

        for side in range(2):
            pl.when(sends_core(d, side))(lambda: core_copy(i, side).wait_send())
        pl.when(sends_pair(d, n))(lambda: pair_copy(i).wait_send())
        pl.when(sends_layer(d, n))(lambda: layer_copy(i).wait_send())

        @pl.when(d == 0)
        def _():
            rep_copy(n).wait_send()
            pl.when(sends_far(n))(lambda: far_copy(n).wait_send())

    for d in range(3):
        for side in range(2):
            pl.when(sends_core(d, side))(lambda: core_part_copy(d, side).wait_send())
        pl.when(sends_pair(d))(lambda: pair_part_copy(d).wait_send())
        if d > 0:
            pl.when(sends_layer(d))(lambda: layer_part_copy(d).wait_send())
    rep_part_copy().wait_send()
    for away in range(1, layers):
        spread(away).wait_send()
    for k in range(3):
        widen(k).wait_send()


def layered_backward(cycle, sent_t, self_t, dense, grads):
    step_count, row_total, _ = dense.shape
    width = sent_t.shape[0]
    part = grads.shape[1:]
    depth = 2 * width // cycle
    pieces = 4
    panel = (width, row_total // pieces)
    bf16, f32 = jnp.bfloat16, jnp.float32
    layers = cycle // LANES
    turns = 3 * pieces
    sems = [
        (turns, 2), (turns,), (2 * pieces,), (pieces,), (3, 2), (3,), (2,), (1,),
        (layers,), (3,), (pieces // 2,),
    ]
    vmem = pl.BlockSpec(memory_space=pltpu.VMEM)
    return pl.pallas_call(
        functools.partial(layered_backward_kernel, cycle, pieces),
        in_specs=[vmem, vmem, pl.BlockSpec(memory_space=pl.ANY), vmem],
        out_specs=[vmem] * 4,
        out_shape=(
            jax.ShapeDtypeStruct((row_total, width), bf16),
            jax.ShapeDtypeStruct((width, width), f32),
            jax.ShapeDtypeStruct((width, width), f32),
            jax.ShapeDtypeStruct((1, width), f32),
        ),
        scratch_shapes=[
            pltpu.VMEM(dense.shape, bf16),
            pltpu.VMEM((turns, 2, *panel), f32),
            pltpu.VMEM((turns, 2, *panel), bf16),
            pltpu.VMEM((turns, 2, *panel), bf16),
            pltpu.VMEM((turns, *panel), bf16),
            pltpu.VMEM((turns, *panel), bf16),
            pltpu.VMEM((2 * pieces, *panel), bf16),
            pltpu.VMEM((2 * pieces, *panel), bf16),
            pltpu.VMEM((pieces, *panel), bf16),
            pltpu.VMEM((pieces, *panel), bf16),
            pltpu.VMEM((pieces // 2, *panel), bf16),
            pltpu.VMEM((pieces // 2, *panel), bf16),
            pltpu.VMEM((3, 2, *part), f32),
            pltpu.VMEM((3, 2, *part), bf16),
            pltpu.VMEM((3, *part), bf16),
            pltpu.VMEM((3, *part), bf16),
            pltpu.VMEM((2, *part), bf16),
            pltpu.VMEM((2, *part), bf16),
            pltpu.VMEM(part, bf16),
            pltpu.VMEM(part, bf16),
            pltpu.VMEM((LANES, layers, depth, width), bf16),
            pltpu.SemaphoreType.DMA((step_count,)),
        ] + [pltpu.SemaphoreType.DMA(shape) for shape in sems for _ in range(2)],
        compiler_params=pltpu.CompilerParams(
            collective_id=3, has_side_effects=True, vmem_limit_bytes=44 * 2**20
        ),
        name="layered_backward",
    )(sent_t, self_t, dense, grads)


def layered_front_kernel(
    cycle, pieces, features, behind, across, dense,
    weight_self, weight_neighbor, bias, cotangent,
    activations, sent_t, self_t, grads,
    slots, blocks, total, rep_out, rep_in, sums, first_sem, block_sem, *sems,
):
    f32, bf16 = jnp.float32, jnp.bfloat16
    steps, rows = blocks.shape[0], blocks.shape[1]
    halves, half = total.shape[0], total.shape[2]
    size = rows // pieces
    at = Spot(cycle, steps)
    lane = at.lane
    diagonal = (1 - at.pair) * 2 + 1 - at.core
    layer_sems, pair_sems, core_sems, relay_sems, rep_sems, far_sems = [
        (sems[2 * k], sems[2 * k + 1]) for k in range(6)
    ]
    by_pair = pieces // 4
    partner = {"rep": 1 - at.replica}
    onward = {"blk": at.at_layer(at.sign)}

    def first(h, k):
        source, place = (
            (features, (0, lane)), (behind, (1, lane)), (across, (0, at.lane_across))
        )[k]
        return pltpu.make_async_copy(
            source.at[:, h * half : (h + 1) * half], slots.at[(*place, h)],
            first_sem.at[h, k],
        )

    for h in range(halves):
        for k in range(3):
            first(h, k).start()

    def load(step):
        return pltpu.make_async_copy(
            dense.at[step], blocks.at[step], block_sem.at[step]
        )

    @pl.loop(0, steps)
    def _(hop):
        load((steps - 1 - hop) * at.replica + hop * (1 - at.replica)).start()

    at.greet()
    for h in range(halves):
        for k in range(3):
            first(h, k).wait()

    def span(piece):
        return pl.ds(pl.multiple_of(piece * size, size), size)

    def layer_copy(h, d, p):
        return remote(slots.at[d, lane, h, span(p)], slots.at[d + 1, lane, h, span(p)],
                      layer_sems, (h, d, p), onward)

    def spot_copy(which, h, d, p):
        whose = at.lane_across if which == "relay" else lane
        here = slots.at[d, whose, h, span(p)]
        pack = {"pair": pair_sems, "core": core_sems, "relay": relay_sems}[which]
        device = at.across if which == "pair" else at.beside
        return remote(here, here, pack, (h, d, p), {"blk": device})

    def rep_copy(h, p):
        return remote(rep_out.at[h, span(p)], rep_in.at[h, span(p)], rep_sems, (h, p),
                      partner)

    def far_copy(h, p):
        whose = at.lane_across
        return remote(slots.at[1, whose, h, span(p)], slots.at[2, whose, h, span(p)],
                      far_sems, (h, p), onward)

    def sends_layer(p):
        return jnp.logical_or(
            at.chip_meets(at.pair, lane, 2),
            jnp.logical_and(p < by_pair, at.layer_meets(lane, 2)),
        )

    def sends_far(p):
        return jnp.logical_and(p >= by_pair, gets["pair"](2))

    def over_pair(d, p, kind):
        holds = kind["pair"](d)
        return jnp.logical_and(p < by_pair, holds) if d == 2 else holds

    sends = {
        "pair": lambda d: at.chip_meets(1 - at.pair, lane, d),
        "core": lambda d: at.meets(at.lane_beside, lane, d),
        "relay": lambda d: at.meets(at.lane_beside, at.lane_across, d),
    }
    gets = {
        "pair": lambda d: at.chip_meets(at.pair, at.lane_across, d),
        "core": lambda d: at.meets(lane, at.lane_beside, d),
        "relay": lambda d: at.meets(lane, diagonal, d),
    }

    def give(h, d, p, kinds):
        if "layer" in kinds:
            pl.when(sends_layer(p))(lambda: layer_copy(h, d, p).start())
        if "pair" in kinds:
            pl.when(over_pair(d, p, sends))(
                lambda: spot_copy("pair", h, d, p).start()
            )
        if "core" in kinds:
            pl.when(sends["core"](d))(lambda: spot_copy("core", h, d, p).start())

    def give_all(h, d, kinds):
        @pl.loop(0, pieces)
        def _(p):
            give(h, d, p, kinds)

    def arrive(h):
        @pl.loop(0, pieces)
        def _(p):
            @pl.when(sends_layer(p))
            def _():
                layer_copy(h, 1, p).wait_recv()
                give(h, 2, p, ("pair", "core"))

    def relay(h, d, then=None):
        @pl.loop(0, pieces)
        def _(p):
            @pl.when(gets["pair"](d))
            def _():
                if d > 0:
                    pl.when(over_pair(d, p, gets))(
                        lambda: spot_copy("pair", h, d, p).wait_recv()
                    )
                if d == 1:
                    pl.when(sends_far(p))(lambda: far_copy(h, p).start())
                if d == 2:
                    pl.when(sends_far(p))(lambda: far_copy(h, p).wait_recv())
                pl.when(sends["relay"](d))(
                    lambda: spot_copy("relay", h, d, p).start()
                )

            if then is not None:
                then(p)

    def gathered(h, d):
        for which in ("core", "relay"):
            @pl.when(gets[which](d))
            def _():
                @pl.loop(0, pieces)
                def _(p):
                    spot_copy(which, h, d, p).wait_recv()

    def multiply(h, d, place):
        @pl.loop(0, LANES)
        def _(source):
            step = at.step(lane, source, d)

            @pl.when(at.meets(lane, source, d))
            def _():
                total[h, place, :] += jnp.dot(
                    blocks[step, place, :], slots[d, source, h],
                    preferred_element_type=f32,
                )

    def await_blocks(d):
        @pl.loop(0, LANES)
        def _(source):
            @pl.when(at.meets(lane, source, d))
            def _():
                load(at.step(lane, source, d)).wait()

    def whole(h, d):
        gathered(h, d)
        if h == 0:
            await_blocks(d)
        multiply(h, d, slice(None))

    def last(h):
        gathered(h, 2)
        if h == 0:
            await_blocks(2)

        @pl.loop(0, pieces)
        def _(p):
            multiply(h, 2, span(p))
            rep_out[h, span(p)] = total[h, span(p)].astype(bf16)
            rep_copy(h, p).start()

    give_all(0, 1, ("layer", "pair", "core"))
    for h in range(halves):
        give_all(h, 0, ("core",))
        relay(h, 0)
    total[...] = jnp.zeros_like(total)
    sums[...] = jnp.zeros_like(sums)
    whole(0, 0)
    relay(0, 1, lambda p: give(1, 1, p, ("pair", "core")))
    give_all(1, 1, ("layer",))
    arrive(0)
    whole(0, 1)
    relay(1, 1)
    relay(0, 2)
    last(0)
    arrive(1)
    whole(1, 0)
    whole(1, 1)
    relay(1, 2)
    last(1)

    def joined(ref, place):
        return jnp.concatenate([ref[h, place] for h in range(halves)], axis=1)

    width = halves * half

    @pl.loop(0, pieces)
    def _(p):
        place = span(p)
        for h in range(halves):
            rep_copy(h, p).wait_recv()
        mine, other = joined(rep_out, place), joined(rep_in, place)
        aggregate = (mine.astype(f32) + other.astype(f32)).astype(bf16)
        own_rows = jnp.concatenate(
            [slots[0, lane, h, place] for h in range(halves)], axis=1
        )
        pre = (
            jnp.dot(own_rows, weight_self[...], preferred_element_type=f32)
            + jnp.dot(aggregate, weight_neighbor[...], preferred_element_type=f32)
            + bias[...]
        )
        sigmoid = jax.nn.sigmoid(pre)
        activations[place, :] = (pre * sigmoid).astype(activations.dtype)
        derivative = sigmoid * (1.0 + pre * (1.0 - sigmoid))
        grad_pre = (cotangent[place, :].astype(f32) * derivative).astype(bf16)
        sent_t[:, place] = lax.dot_general(
            weight_neighbor[...], grad_pre, COLS_COLS, preferred_element_type=f32
        ).astype(sent_t.dtype)
        self_t[:, place] = lax.dot_general(
            weight_self[...], grad_pre, COLS_COLS, preferred_element_type=f32
        )
        sums[0:width] += lax.dot_general(
            own_rows, grad_pre, ROWS_ROWS, preferred_element_type=f32
        )
        sums[width : 2 * width] += lax.dot_general(
            aggregate, grad_pre, ROWS_ROWS, preferred_element_type=f32
        )
        sums[2 * width : 2 * width + 1] += jnp.sum(
            grad_pre.astype(f32), axis=0, keepdims=True
        )

    parts = grads.shape[0]
    depth = 2 * width // parts
    tail = grads.shape[1] - depth
    bias_rows = jnp.broadcast_to(
        sums[2 * width : 2 * width + 1], (tail, width)
    ).astype(grads.dtype)
    for part in range(parts):
        grads[part, 0:depth, :] = sums[part * depth : (part + 1) * depth].astype(
            grads.dtype
        )
        grads[part, depth:, :] = bias_rows

    @pl.loop(0, pieces)
    def _(p):
        for h in range(halves):
            for d in range(3):
                if d == 1:
                    pl.when(sends_layer(p))(lambda: layer_copy(h, d, p).wait_send())
                    pl.when(sends_far(p))(lambda: far_copy(h, p).wait_send())
                if d > 0:
                    pl.when(over_pair(d, p, sends))(
                        lambda: spot_copy("pair", h, d, p).wait_send()
                    )
                for which in ("core", "relay"):
                    pl.when(sends[which](d))(
                        lambda: spot_copy(which, h, d, p).wait_send()
                    )
            rep_copy(h, p).wait_send()


def ahead_of_build(cycle, features):
    layers, places = cycle // LANES, [(g, r) for g in range(cycle) for r in range(2)]
    behind, across = [], []
    for group, replica in places:
        sign = 1 - 2 * replica
        layer, lane = group // LANES, group % LANES
        target = (layer + sign) % layers * LANES + lane
        behind.append((group * 2 + replica, target * 2 + replica))
        if lane // 2 == replica:
            target = layer * LANES + (lane + 2) % LANES
            across.append((group * 2 + replica, target * 2 + replica))
    return [lax.ppermute(features, ("blk", "rep"), pairs) for pairs in (behind, across)]


def layered_front(
    cycle, features, behind, across, dense, weight_self, weight_neighbor, bias, cotangent
):
    step_count, row_total, _ = dense.shape
    width = features.shape[1]
    pieces, halves = 4, 2
    half = width // halves
    bf16, f32 = jnp.bfloat16, jnp.float32
    shape = jax.ShapeDtypeStruct
    vmem, anywhere = [
        pl.BlockSpec(memory_space=space) for space in (pltpu.VMEM, pl.ANY)
    ]
    sems = [(halves, 3, pieces)] * 4 + [(halves, pieces)] * 2
    return pl.pallas_call(
        functools.partial(layered_front_kernel, cycle, pieces),
        in_specs=[anywhere] * 4 + [vmem] * 4,
        out_specs=[vmem] * 4,
        out_shape=(
            shape((row_total, width), bf16),
            shape((width, row_total), bf16),
            shape((width, row_total), f32),
            shape((cycle, 2 * width // cycle + 16, width), bf16),
        ),
        scratch_shapes=[
            pltpu.VMEM((3, LANES, halves, row_total, half), bf16),
            pltpu.VMEM(dense.shape, bf16),
            pltpu.VMEM((halves, row_total, half), f32),
            pltpu.VMEM((halves, row_total, half), bf16),
            pltpu.VMEM((halves, row_total, half), bf16),
            pltpu.VMEM((2 * width + 8, width), f32),
            pltpu.SemaphoreType.DMA((halves, 3)),
            pltpu.SemaphoreType.DMA((step_count,)),
        ] + [pltpu.SemaphoreType.DMA(size) for size in sems for _ in range(2)],
        compiler_params=pltpu.CompilerParams(
            collective_id=4, has_side_effects=True, vmem_limit_bytes=36 * 2**20
        ),
        name="layered_front",
    )(features, behind, across, dense, weight_self, weight_neighbor, bias, cotangent)


def close_kernel(*refs):
    count = len(refs) // 2
    for source, target in zip(refs[:count], refs[count:]):
        target[...] = source[...]


def close(arrays):
    return pl.pallas_call(
        close_kernel,
        out_shape=tuple(jax.ShapeDtypeStruct(a.shape, a.dtype) for a in arrays),
        compiler_params=pltpu.CompilerParams(vmem_limit_bytes=8 * 2**20),
        name="close",
    )(*arrays)


def on_device(
    features,
    weight_self,
    weight_neighbor,
    bias_vector,
    tile_row,
    tile_column,
    tile_value,
    tile_count,
    tile_table,
    cotangent,
):
    f32, bf16 = jnp.float32, jnp.bfloat16
    cycle_length = lax.axis_size("blk")
    replicas = lax.axis_size("rep")
    step_count = cycle_length // replicas
    replica = lax.axis_index("rep")
    row_total, width = features.shape

    jump = jnp.minimum(replica, replicas - 1 - replica)
    jump_bits = max(replicas // 2 - 1, 0).bit_length()
    reverse = (2 * replica) // replicas

    def shifted(array, sign):
        for bit in range(jump_bits):
            by = sign * (step_count << bit)
            moved = jnp.where(
                reverse == 0,
                lax.ppermute(
                    array, "blk",
                    [(i, (i + by) % cycle_length) for i in range(cycle_length)],
                ),
                lax.ppermute(
                    array, "blk",
                    [(i, (i - by) % cycle_length) for i in range(cycle_length)],
                ),
            )
            array = jnp.where(jump // (1 << bit) % 2 == 1, moved, array)
        return array

    if is_layered(cycle_length, replicas):
        early = ahead_of_build(cycle_length, features)
    dense = build_dense(
        tile_row[0], tile_column[0], tile_value[0], tile_count[0], tile_table, row_total
    )
    if is_layered(cycle_length, replicas):
        activations, sent_t, self_t, grads = layered_front(
            cycle_length, features, *early, dense, weight_self, weight_neighbor,
            bias_vector.reshape(1, width), cotangent,
        )
        results = close((
            activations, *layered_backward(cycle_length, sent_t, self_t, dense, grads)
        ))
        return (*results[:4], results[4][0])
    mine = forward(cycle_length, replicas, shifted(features, 1), dense)
    bit = 1
    while True:
        other = lax.ppermute(mine, "rep", [(i, i ^ bit) for i in range(replicas)])
        bit *= 2
        if bit >= replicas:
            break
        mine = (mine.astype(f32) + other.astype(f32)).astype(bf16)
    activations, sent_t, self_t, grads = layer(
        cycle_length, features, mine, other, weight_self, weight_neighbor,
        bias_vector.reshape(1, width), cotangent,
    )
    pushed, part = backward(cycle_length, replicas, sent_t, dense, grads)
    pushed, part = shifted(pushed, -1), shifted(part, -1)

    def over_replicas(array):
        bit = 1
        while 2 * bit < replicas:
            other = lax.ppermute(array, "rep", [(i, i ^ bit) for i in range(replicas)])
            array = (array.astype(f32) + other.astype(f32)).astype(bf16)
            bit *= 2
        return array

    weights, bias_rows, grad_t = finish(
        cycle_length, replicas, over_replicas(pushed), over_replicas(part), self_t
    )
    weights = weights.reshape(2 * width, width)
    grad_features = grad_t.T
    return (
        activations,
        grad_features,
        weights[:width],
        weights[width:],
        bias_rows[0],
    )


def solution(mesh):
    placed = (
        P("blk", None),
        P(),
        P(),
        P(),
        P("blk", "rep", None),
        P("blk", "rep", None),
        P("blk", "rep", None),
        P("blk", "rep"),
        P(("blk", "rep"), None, None),
        P("blk", None),
    )
    return jax.shard_map(
        on_device,
        mesh=mesh,
        in_specs=placed,
        out_specs=(P("blk", None), P("blk", None), P(), P(), P()),
        check_vma=False,
    )
```

```python
import functools

import jax
import jax.numpy as jnp
from jax import lax
from jax.experimental import pallas as pl
from jax.experimental.pallas import tpu as pltpu
from jax.sharding import PartitionSpec as P

ROWS_ROWS = (((0,), (0,)), ((), ()))
COLS_COLS = (((1,), (1,)), ((), ()))


def build_kernel(rows, columns, values, counts, table, dense):
    step = pl.program_id(0)
    tile = table.shape[1]
    dense[...] = jnp.zeros_like(dense)

    def add_tile(slot, carry):
        row = pl.multiple_of(rows[step, slot] * tile, tile)
        column = pl.multiple_of(columns[step, slot] * tile, tile)
        place = (0, pl.ds(row, tile), pl.ds(column, tile))
        dense[place] = dense[place] + table[values[step, slot]]
        return carry

    lax.fori_loop(0, counts[step], add_tile, 0)


def build_dense(rows, columns, values, counts, table, row_total):
    step_count = rows.shape[0]
    return pl.pallas_call(
        build_kernel,
        grid_spec=pltpu.PrefetchScalarGridSpec(
            num_scalar_prefetch=4,
            grid=(step_count,),
            in_specs=[pl.BlockSpec(table.shape, lambda s, *_: (0, 0, 0))],
            out_specs=pl.BlockSpec((1, row_total, row_total), lambda s, *_: (s, 0, 0)),
        ),
        out_shape=jax.ShapeDtypeStruct((step_count, row_total, row_total), jnp.bfloat16),
        cost_estimate=pl.CostEstimate(
            flops=0, bytes_accessed=20 * 2**20, transcendentals=0
        ),
        name="build",
    )(rows, columns, values, counts, table)


def ring_place(cycle, replicas):
    group = lax.axis_index("blk")
    replica = lax.axis_index("rep")
    reverse = (2 * replica) // replicas if replicas > 1 else 0 * replica
    ahead = lax.rem(group + 1 - 2 * reverse + cycle, cycle)
    behind = lax.rem(group - 1 + 2 * reverse + cycle, cycle)
    return group, replica, reverse, ahead, behind


def greet(devices):
    barrier = pltpu.get_barrier_semaphore()
    for device in devices:
        pl.semaphore_signal(
            barrier, inc=1, device_id={"blk": device},
            device_id_type=pl.DeviceIdType.MESH,
        )
    pl.semaphore_wait(barrier, len(devices))


def forward_kernel(
    cycle, replicas, pieces, features, dense, out,
    slots, blocks, total, block_sem, first_sem, send_sem, recv_sem,
):
    steps, rows = blocks.shape[0], blocks.shape[1]
    _, _, reverse, ahead, behind = ring_place(cycle, replicas)
    size = rows // pieces
    first = pltpu.make_async_copy(features, slots.at[0], first_sem)
    first.start()

    def load(step):
        return pltpu.make_async_copy(
            dense.at[step], blocks.at[step], block_sem.at[step]
        )

    def in_order(hop):
        return hop * (1 - reverse) + (steps - hop) * reverse

    @pl.loop(0, steps)
    def _(hop):
        load(in_order(hop + reverse)).start()

    greet((ahead, behind))
    first.wait()

    def hop_copy(hop, piece):
        span = pl.ds(piece * size, size)
        return pltpu.make_async_remote_copy(
            src_ref=slots.at[hop, span],
            dst_ref=slots.at[hop + 1, span],
            send_sem=send_sem.at[hop, piece],
            recv_sem=recv_sem.at[hop, piece],
            device_id={"blk": ahead},
            device_id_type=pl.DeviceIdType.MESH,
        )

    total[...] = jnp.zeros_like(total)
    hops = steps - 1 + reverse

    @pl.loop(0, hops + 1)
    def _(hop):
        for piece in range(pieces):
            @pl.when(hop > 0)
            def _():
                hop_copy(hop - 1, piece).wait_recv()

            @pl.when(hop < hops)
            def _():
                hop_copy(hop, piece).start()

        step = in_order(hop)

        @pl.when(step < steps)
        def _():
            load(step).wait()
            total[...] += jnp.dot(
                blocks[step], slots[hop], preferred_element_type=jnp.float32
            )

    out[...] = total[...].astype(out.dtype)

    @pl.loop(0, hops)
    def _(hop):
        for piece in range(pieces):
            hop_copy(hop, piece).wait_send()


LANES = 4


def is_layered(cycle, replicas):
    return (
        cycle // replicas == 2 * LANES and cycle >= 3 * LANES
        and cycle % LANES == 0 and replicas == 2
    )


def forward(cycle, replicas, features, dense):
    step_count, row_total, _ = dense.shape
    width = features.shape[1]
    pieces = 4
    slots, sems = (step_count + 1, row_total, width), (step_count, pieces)
    return pl.pallas_call(
        functools.partial(forward_kernel, cycle, replicas, pieces),
        in_specs=[pl.BlockSpec(memory_space=pl.ANY)] * 2,
        out_specs=pl.BlockSpec(memory_space=pltpu.VMEM),
        out_shape=jax.ShapeDtypeStruct((row_total, width), jnp.bfloat16),
        scratch_shapes=[
            pltpu.VMEM(slots, jnp.bfloat16),
            pltpu.VMEM(dense.shape, jnp.bfloat16),
            pltpu.VMEM((row_total, width), jnp.float32),
            pltpu.SemaphoreType.DMA((step_count,)),
            pltpu.SemaphoreType.DMA,
            pltpu.SemaphoreType.DMA(sems),
            pltpu.SemaphoreType.DMA(sems),
        ],
        compiler_params=pltpu.CompilerParams(collective_id=0, has_side_effects=True),
        name="forward",
    )(features, dense)


def layer_kernel(
    features, mine, other, weight_self, weight_neighbor, bias, cotangent,
    activations, sent_t, self_t, grads,
):
    f32 = jnp.float32
    width = features.shape[1]
    aggregate = (mine[...].astype(f32) + other[...].astype(f32)).astype(jnp.bfloat16)
    pre = (
        jnp.dot(features[...], weight_self[...], preferred_element_type=f32)
        + jnp.dot(aggregate, weight_neighbor[...], preferred_element_type=f32)
        + bias[...]
    )
    sigmoid = jax.nn.sigmoid(pre)
    activations[...] = (pre * sigmoid).astype(activations.dtype)
    derivative = sigmoid * (1.0 + pre * (1.0 - sigmoid))
    grad_pre = (cotangent[...].astype(f32) * derivative).astype(jnp.bfloat16)
    sent_t[...] = lax.dot_general(
        weight_neighbor[...], grad_pre, COLS_COLS, preferred_element_type=f32
    ).astype(sent_t.dtype)
    self_t[...] = lax.dot_general(
        weight_self[...], grad_pre, COLS_COLS, preferred_element_type=f32
    )
    grad_self = lax.dot_general(
        features[...], grad_pre, ROWS_ROWS, preferred_element_type=f32
    ).astype(grads.dtype)
    grad_neighbor = lax.dot_general(
        aggregate, grad_pre, ROWS_ROWS, preferred_element_type=f32
    ).astype(grads.dtype)
    summed = jnp.sum(grad_pre.astype(f32), axis=0, keepdims=True)
    parts = grads.shape[0]
    depth = 2 * width // parts
    tail = grads.shape[1] - depth
    bias_rows = jnp.broadcast_to(summed, (tail, width)).astype(grads.dtype)
    for part in range(parts):
        source, place = (
            (grad_self, part) if 2 * part < parts else (grad_neighbor, part - parts // 2)
        )
        grads[part, 0:depth, :] = source[place * depth : (place + 1) * depth, :]
        grads[part, depth:, :] = bias_rows


def layer(parts, features, mine, other, weight_self, weight_neighbor, bias, cotangent):
    row_total, width = features.shape
    shape = jax.ShapeDtypeStruct
    return pl.pallas_call(
        layer_kernel,
        out_shape=(
            shape((row_total, width), jnp.bfloat16),
            shape((width, row_total), jnp.bfloat16),
            shape((width, row_total), jnp.float32),
            shape((parts, 2 * width // parts + 16, width), jnp.bfloat16),
        ),
        name="layer",
    )(features, mine, other, weight_self, weight_neighbor, bias, cotangent)


def backward_kernel(
    cycle, replicas, pieces, sent_t, dense, grads, out, part_out,
    landed, held, part_landed, part_held, blocks, term,
    block_sem, send_sem, recv_sem,
):
    steps = blocks.shape[0]
    width = sent_t.shape[0]
    size = width // pieces
    f32 = jnp.float32
    group, replica, reverse, behind, ahead = ring_place(cycle, replicas)

    def load(step):
        return pltpu.make_async_copy(
            dense.at[step], blocks.at[step], block_sem.at[step]
        )

    def in_order(hop):
        return (steps - 1 - hop) * (1 - reverse) + hop * reverse

    @pl.loop(0, steps)
    def _(hop):
        load(in_order(hop)).start()

    greet((ahead, behind))

    def hop_copy(hop, piece):
        if piece < pieces:
            span = pl.ds(piece * size, size)
            source, target = held.at[hop, span], landed.at[hop, span]
        else:
            source, target = part_held.at[hop], part_landed.at[hop]
        return pltpu.make_async_remote_copy(
            src_ref=source,
            dst_ref=target,
            send_sem=send_sem.at[hop, piece],
            recv_sem=recv_sem.at[hop, piece],
            device_id={"blk": ahead},
            device_id_type=pl.DeviceIdType.MESH,
        )

    hops = steps - 1 + reverse

    @pl.loop(0, steps)
    def _(hop):
        step = in_order(hop)
        target = lax.rem(group - steps * replica - step + 2 * cycle, cycle)
        load(step).wait()
        term[...] = jnp.dot(sent_t[...], blocks[step], preferred_element_type=f32)
        for piece in range(pieces + 1):
            span = pl.ds(piece * size, size)

            @pl.when(hop > 0)
            def _():
                hop_copy(hop - 1, piece).wait_recv()
                if piece < pieces:
                    held[hop, span] = (
                        term[span] + landed[hop - 1, span].astype(f32)
                    ).astype(held.dtype)
                else:
                    part_held[hop] = (
                        grads[target].astype(f32) + part_landed[hop - 1].astype(f32)
                    ).astype(part_held.dtype)

            @pl.when(hop == 0)
            def _():
                if piece < pieces:
                    held[hop, span] = term[span].astype(held.dtype)
                else:
                    part_held[hop] = grads[target]

            @pl.when(hop < hops)
            def _():
                hop_copy(hop, piece).start()

    @pl.when(reverse == 0)
    def _():
        out[...] = held[steps - 1]
        part_out[...] = part_held[steps - 1]

    @pl.when(reverse == 1)
    def _():
        for piece in range(pieces + 1):
            hop_copy(steps - 1, piece).wait_recv()
        out[...] = landed[steps - 1]
        part_out[...] = part_landed[steps - 1]

    @pl.loop(0, hops)
    def _(hop):
        for piece in range(pieces + 1):
            hop_copy(hop, piece).wait_send()


def backward(cycle, replicas, sent_t, dense, grads):
    step_count, row_total, _ = dense.shape
    width = sent_t.shape[0]
    part = grads.shape[1:]
    pieces = 4
    bf16 = jnp.bfloat16
    return pl.pallas_call(
        functools.partial(backward_kernel, cycle, replicas, pieces),
        in_specs=[
            pl.BlockSpec(memory_space=pltpu.VMEM),
            pl.BlockSpec(memory_space=pl.ANY),
            pl.BlockSpec(memory_space=pltpu.VMEM),
        ],
        out_specs=[pl.BlockSpec(memory_space=pltpu.VMEM)] * 2,
        out_shape=(
            jax.ShapeDtypeStruct((width, row_total), bf16),
            jax.ShapeDtypeStruct(part, bf16),
        ),
        scratch_shapes=[
            pltpu.VMEM((step_count, width, row_total), bf16),
            pltpu.VMEM((step_count, width, row_total), bf16),
            pltpu.VMEM((step_count, *part), bf16),
            pltpu.VMEM((step_count, *part), bf16),
            pltpu.VMEM(dense.shape, bf16),
            pltpu.VMEM((width, row_total), jnp.float32),
            pltpu.SemaphoreType.DMA((step_count,)),
            pltpu.SemaphoreType.DMA((step_count, pieces + 1)),
            pltpu.SemaphoreType.DMA((step_count, pieces + 1)),
        ],
        compiler_params=pltpu.CompilerParams(collective_id=1, has_side_effects=True),
        name="backward",
    )(sent_t, dense, grads)


def finish_kernel(
    cycle, replicas, pushed, part, self_t, weights, bias_out, grad_t,
    gathered, landed, part_landed, pair_send, pair_recv, send_sem, recv_sem,
):
    f32 = jnp.float32
    depth = gathered.shape[1]
    group = lax.axis_index("blk")
    partner = {"rep": lax.rem(lax.axis_index("rep") + replicas // 2, replicas)}
    mesh_id = pl.DeviceIdType.MESH
    barrier = pltpu.get_barrier_semaphore()
    pl.semaphore_signal(barrier, inc=1, device_id=partner, device_id_type=mesh_id)
    for away in range(1, cycle):
        pl.semaphore_signal(
            barrier, inc=1, device_id={"blk": lax.rem(group + away, cycle)},
            device_id_type=mesh_id,
        )
    pl.semaphore_wait(barrier, cycle)

    def swap(source, target, index):
        return pltpu.make_async_remote_copy(
            src_ref=source, dst_ref=target,
            send_sem=pair_send.at[index], recv_sem=pair_recv.at[index],
            device_id=partner, device_id_type=mesh_id,
        )

    part_swap = swap(part, part_landed, 0)
    part_swap.start()
    panel_swap = swap(pushed, landed, 1)
    panel_swap.start()
    part_swap.wait()
    summed = part[...].astype(f32) + part_landed[...].astype(f32)
    bias_out[...] = summed[depth:]
    gathered[group] = summed[:depth].astype(gathered.dtype)

    def put(away):
        return pltpu.make_async_remote_copy(
            src_ref=gathered.at[group],
            dst_ref=gathered.at[group],
            send_sem=send_sem.at[away],
            recv_sem=recv_sem.at[away],
            device_id={"blk": lax.rem(group + away, cycle)},
            device_id_type=mesh_id,
        )

    @pl.loop(1, cycle)
    def _(away):
        put(away).start()

    @pl.loop(1, cycle)
    def _(away):
        put(away).wait()

    weights[...] = gathered[...].astype(f32)
    panel_swap.wait()
    grad_t[...] = (
        self_t[...] + (pushed[...].astype(f32) + landed[...].astype(f32))
    ).astype(grad_t.dtype)


def finish(cycle, replicas, pushed, part, self_t):
    width = pushed.shape[0]
    depth = 2 * width // cycle
    tail = part.shape[0] - depth
    shape = jax.ShapeDtypeStruct
    return pl.pallas_call(
        functools.partial(finish_kernel, cycle, replicas),
        in_specs=[pl.BlockSpec(memory_space=pltpu.VMEM)] * 3,
        out_specs=[pl.BlockSpec(memory_space=pltpu.VMEM)] * 3,
        out_shape=(
            shape((cycle, depth, width), jnp.float32),
            shape((tail, width), jnp.float32),
            shape(pushed.shape, jnp.bfloat16),
        ),
        scratch_shapes=[
            pltpu.VMEM((cycle, depth, width), jnp.bfloat16),
            pltpu.VMEM(pushed.shape, jnp.bfloat16),
            pltpu.VMEM(part.shape, jnp.bfloat16),
            pltpu.SemaphoreType.DMA((2,)),
            pltpu.SemaphoreType.DMA((2,)),
            pltpu.SemaphoreType.DMA((cycle,)),
            pltpu.SemaphoreType.DMA((cycle,)),
        ],
        compiler_params=pltpu.CompilerParams(collective_id=2, has_side_effects=True),
        name="finish",
    )(pushed, part, self_t)


class Spot:
    def __init__(self, cycle, steps):
        self.steps, self.layers = steps, cycle // LANES
        self.group, self.replica = lax.axis_index("blk"), lax.axis_index("rep")
        self.sign = 1 - 2 * self.replica
        self.layer, self.lane = self.group // LANES, lax.rem(self.group, LANES)
        self.pair, self.core = self.lane // 2, lax.rem(self.lane, 2)
        self.lane_across = (1 - self.pair) * 2 + self.core
        self.lane_beside = self.pair * 2 + 1 - self.core
        self.across = self.layer * LANES + self.lane_across
        self.beside = self.layer * LANES + self.lane_beside

    def layer_at(self, distance):
        return lax.rem(self.layer + distance + 2 * self.layers, self.layers)

    def at_layer(self, distance):
        return self.layer_at(distance) * LANES + self.lane

    def step(self, lane, other_lane, distance):
        return (
            self.replica * self.steps + lane - other_lane
            + self.sign * LANES * distance
        )

    def meets(self, lane, other_lane, distance):
        step = self.step(lane, other_lane, distance)
        return jnp.logical_and(step >= 0, step < self.steps)

    def chip_meets(self, pair, other_lane, distance):
        return jnp.logical_or(
            self.meets(2 * pair, other_lane, distance),
            self.meets(2 * pair + 1, other_lane, distance),
        )

    def layer_meets(self, other_lane, distance):
        return jnp.logical_or(
            self.chip_meets(0, other_lane, distance),
            self.chip_meets(1, other_lane, distance),
        )

    def greet(self):
        barrier = pltpu.get_barrier_semaphore()
        signal = functools.partial(
            pl.semaphore_signal, barrier, inc=1, device_id_type=pl.DeviceIdType.MESH
        )
        signal(device_id={"blk": self.across})
        signal(device_id={"blk": self.beside})
        signal(device_id={"rep": 1 - self.replica})
        for away in range(1, self.layers):
            signal(device_id={"blk": self.at_layer(away)})
        pl.semaphore_wait(barrier, 2 + self.layers)


def remote(source, target, sems, index, device):
    send, recv = sems
    return pltpu.make_async_remote_copy(
        src_ref=source, dst_ref=target,
        send_sem=send.at[index], recv_sem=recv.at[index],
        device_id=device, device_id_type=pl.DeviceIdType.MESH,
    )


def backward_part(
    cycle, pieces, weight_self, sent_t, grad_pre, blocks, grads, fill_grads,
    grad_out, weight_self_out, weight_neighbor_out, bias_out,
    acc, core_out, core_in, pair_out, pair_in, layer_out, layer_in,
    rep_out, rep_in, far_out, far_in, part_acc, core_part, pair_part_out, pair_part,
    layer_part_out, layer_part, rep_part_out, rep_part, gathered, *sems,
):
    f32 = jnp.float32
    bf16 = jnp.bfloat16
    steps, rows = blocks.shape[0], blocks.shape[1]
    size = rows // pieces
    at = Spot(cycle, steps)
    layers = at.layers
    depth = gathered.shape[2]
    (core_sems, pair_sems, layer_sems, rep_sems, core_part_sems, pair_part_sems,
     layer_part_sems, rep_part_sems, spread_sems, widen_sems, far_sems) = [
        (sems[2 * k], sems[2 * k + 1]) for k in range(11)
    ]
    by_layer = 1
    partner = {"rep": 1 - at.replica}
    onward = {"blk": at.at_layer(-at.sign)}

    def own_lane(side):
        return 2 * side + at.core

    def other_lane(side):
        return 2 * side + 1 - at.core

    def span(n):
        return pl.ds(pl.multiple_of(n * size, size), size)

    def core_copy(i, side):
        return remote(core_out.at[i, side], core_in.at[i, side], core_sems, (i, side),
                      {"blk": at.beside})

    def pair_copy(i):
        return remote(pair_out.at[i], pair_in.at[i], pair_sems, i, {"blk": at.across})

    def layer_copy(i):
        return remote(layer_out.at[i], layer_in.at[i], layer_sems, i, onward)

    def far_copy(n):
        return remote(far_out.at[n], far_in.at[n], far_sems, n, onward)

    def rep_copy(n):
        return remote(rep_out.at[n], rep_in.at[n], rep_sems, n, partner)

    def part_of(d, lane):
        return at.layer_at(-at.sign * d) * LANES + lane

    def core_part_copy(d, side):
        return remote(grads.at[part_of(d, other_lane(side))], core_part.at[d, side],
                      core_part_sems, (d, side), {"blk": at.beside})

    def pair_part_copy(d):
        return remote(pair_part_out.at[d], pair_part.at[d], pair_part_sems, d,
                      {"blk": at.across})

    def layer_part_copy(d):
        return remote(layer_part_out.at[d - 1], layer_part.at[d - 1], layer_part_sems,
                      d - 1, onward)

    def rep_part_copy():
        return remote(rep_part_out, rep_part, rep_part_sems, 0, partner)

    def spread(away):
        here = gathered.at[at.lane, at.layer]
        return remote(here, here, spread_sems, away, {"blk": at.at_layer(away)})

    def widen(k):
        lane = at.lane_across if k == 2 else at.lane
        device = at.across if k == 0 else at.beside
        return remote(gathered.at[lane], gathered.at[lane], widen_sems, k,
                      {"blk": device})

    def sends_core(d, side):
        return at.meets(at.lane, other_lane(side), d)

    def gets_core(d, side):
        return at.meets(at.lane_beside, own_lane(side), d)

    def early(d, n):
        return jnp.logical_and(d == 2, n < by_layer)

    def sends_far(n):
        return jnp.logical_and(n < by_layer, at.chip_meets(at.pair, at.lane_across, 2))

    def sends_pair(d, n=None):
        here = at.chip_meets(at.pair, at.lane_across, d)
        if n is None:
            return here
        return jnp.logical_and(here, jnp.logical_not(early(d, n)))

    def gets_pair(d, n=None):
        there = at.chip_meets(1 - at.pair, at.lane, d)
        if n is None:
            return there
        return jnp.logical_and(there, jnp.logical_not(early(d, n)))

    def sends_layer(d, n=None):
        far = at.layer_meets(at.lane, 2)
        if n is not None:
            far = jnp.logical_or(
                at.chip_meets(at.pair, at.lane, 2),
                jnp.logical_and(far, n >= by_layer),
            )
        return jnp.logical_and(d > 0, jnp.logical_or(d == 1, far))

    def gets_layer(d, n):
        return jnp.logical_and(d < 2, sends_layer(d + 1, n))

    def product(i, d, n, lane, store):
        step = at.step(at.lane, lane, d)
        wide = pl.ds(pl.multiple_of(n * size, 2 * size), 2 * size)
        value = jnp.dot(
            sent_t[...], blocks[step, :, wide], preferred_element_type=f32
        )
        store(i, value[:, :size])
        store(i + 1, value[:, size:])

    def begin(i):
        d, n = 2 - i // pieces, lax.rem(i, pieces)
        for side in range(2):
            @pl.when(sends_core(d, side))
            def _():
                def store(i, value):
                    core_out[i, side] = value.astype(bf16)

                product(i, d, n, other_lane(side), store)
                core_copy(i, side).start()
                core_copy(i + 1, side).start()

        for side in range(2):
            own = at.meets(at.lane, own_lane(side), d)

            @pl.when(own)
            def _():
                def store(i, value):
                    acc[i, side] = value

                product(i, d, n, own_lane(side), store)

            @pl.when(jnp.logical_not(own))
            def _():
                for k in range(2):
                    acc[i + k, side] = jnp.zeros(acc.shape[2:], f32)

    def over_pair(i):
        d, n = 2 - i // pieces, lax.rem(i, pieces)
        for side in range(2):
            @pl.when(gets_core(d, side))
            def _():
                core_copy(i, side).wait_recv()
                acc[i, side] += core_in[i, side].astype(f32)

        @pl.when(jnp.logical_and(d == 2, sends_far(n)))
        def _():
            far_out[n] = acc[i, 1 - at.pair].astype(bf16)
            far_copy(n).start()

        @pl.when(jnp.logical_and(d == 1, sends_far(n)))
        def _():
            far_copy(n).wait_recv()
            acc[i, 1 - at.pair] += far_in[n].astype(f32)

        @pl.when(sends_pair(d, n))
        def _():
            pair_out[i] = acc[i, 1 - at.pair].astype(bf16)
            pair_copy(i).start()

    def over_layers(i):
        d, n = 2 - i // pieces, lax.rem(i, pieces)

        @pl.when(gets_pair(d, n))
        def _():
            pair_copy(i).wait_recv()
            acc[i, at.pair] += pair_in[i].astype(f32)

        @pl.when(gets_layer(d, n))
        def _():
            layer_copy(i - pieces).wait_recv()
            acc[i, at.pair] += layer_in[i - pieces].astype(f32)

        @pl.when(sends_layer(d, n))
        def _():
            layer_out[i] = acc[i, at.pair].astype(bf16)
            layer_copy(i).start()

        @pl.when(d == 0)
        def _():
            rep_out[n] = acc[i, at.pair].astype(bf16)
            rep_copy(n).start()

            @pl.when(n > 0)
            def _():
                close(n - 1)

    def parts_to_core():
        fill_grads()
        for d in range(3):
            for side in range(2):
                pl.when(sends_core(d, side))(
                    lambda: core_part_copy(d, side).start()
                )

    def parts_to_pair():
        for d in range(3):
            for side in range(2):
                own = at.meets(at.lane, own_lane(side), d)
                part_acc[d, side] = grads[part_of(d, own_lane(side))].astype(
                    f32
                ) * own.astype(f32)

                @pl.when(gets_core(d, side))
                def _():
                    core_part_copy(d, side).wait_recv()
                    part_acc[d, side] += core_part[d, side].astype(f32)

            @pl.when(sends_pair(d))
            def _():
                pair_part_out[d] = part_acc[d, 1 - at.pair].astype(bf16)
                pair_part_copy(d).start()

    def part_onward(d):
        @pl.when(gets_pair(d))
        def _():
            pair_part_copy(d).wait_recv()
            part_acc[d, at.pair] += pair_part[d].astype(f32)

        if d < 2:
            @pl.when(sends_layer(d + 1))
            def _():
                layer_part_copy(d + 1).wait_recv()
                part_acc[d, at.pair] += layer_part[d].astype(f32)

        if d > 0:
            @pl.when(sends_layer(d))
            def _():
                layer_part_out[d - 1] = part_acc[d, at.pair].astype(bf16)
                layer_part_copy(d).start()
        else:
            rep_part_out[...] = part_acc[0, at.pair].astype(bf16)
            rep_part_copy().start()

    def part_spread():
        rep_part_copy().wait_recv()
        summed = rep_part_out[...].astype(f32) + rep_part[...].astype(f32)
        bias_out[...] = summed[depth : depth + 1]
        gathered[at.lane, at.layer] = summed[:depth].astype(bf16)
        for away in range(1, layers):
            spread(away).start()

    def part_over_pair():
        for away in range(1, layers):
            spread(away).wait_recv()
        widen(0).start()

    def part_over_core():
        widen(0).wait_recv()
        widen(1).start()
        widen(2).start()

    def close(n):
        rep_copy(n).wait_recv()
        pushed = rep_out[n].astype(f32) + rep_in[n].astype(f32)
        own = lax.dot_general(
            grad_pre[span(n), :], weight_self[...], COLS_COLS, preferred_element_type=f32
        )
        grad_out[span(n), :] = (own + pushed.T).astype(grad_out.dtype)

    timetable = (
        (1, parts_to_core),
        (3, parts_to_pair),
        (pieces + 2, functools.partial(part_onward, 2)),
        (2 * pieces + 1, functools.partial(part_onward, 1)),
        (2 * pieces + 3, functools.partial(part_onward, 0)),
        (3 * pieces, part_spread),
        (3 * pieces + 2, part_over_pair),
        (3 * pieces + 3, part_over_core),
    )

    @pl.loop(0, 4 * pieces)
    def _(i):
        @pl.when(jnp.logical_and(i > 0, i <= 3 * pieces))
        def _():
            over_pair(i - 1)

        @pl.when(i >= pieces)
        def _():
            over_layers(i - pieces)

        @pl.when(jnp.logical_and(i < 3 * pieces, lax.rem(i, 2) == 0))
        def _():
            begin(i)

        for turn, act in timetable:
            pl.when(i == turn)(act)

    widen(1).wait_recv()
    widen(2).wait_recv()
    per_weight = cycle // 2
    for layer in range(layers):
        for lane in range(LANES):
            part = layer * LANES + lane
            out = weight_self_out if part < per_weight else weight_neighbor_out
            place = part % per_weight * depth
            out[place : place + depth, :] = gathered[lane, layer].astype(f32)
    close(pieces - 1)

    @pl.loop(0, 3 * pieces)
    def _(i):
        d, n = 2 - i // pieces, lax.rem(i, pieces)

        for side in range(2):
            pl.when(sends_core(d, side))(lambda: core_copy(i, side).wait_send())
        pl.when(sends_pair(d, n))(lambda: pair_copy(i).wait_send())
        pl.when(sends_layer(d, n))(lambda: layer_copy(i).wait_send())

        @pl.when(d == 0)
        def _():
            rep_copy(n).wait_send()
            pl.when(sends_far(n))(lambda: far_copy(n).wait_send())

    for d in range(3):
        for side in range(2):
            pl.when(sends_core(d, side))(lambda: core_part_copy(d, side).wait_send())
        pl.when(sends_pair(d))(lambda: pair_part_copy(d).wait_send())
        if d > 0:
            pl.when(sends_layer(d))(lambda: layer_part_copy(d).wait_send())
    rep_part_copy().wait_send()
    for away in range(1, layers):
        spread(away).wait_send()
    for k in range(3):
        widen(k).wait_send()


def backward_scratch(cycle, pieces, row_total, width, part):
    depth = 2 * width // cycle
    panel = (width, row_total // pieces)
    bf16, f32 = jnp.bfloat16, jnp.float32
    layers = cycle // LANES
    turns = 3 * pieces
    sems = [
        (turns, 2), (turns,), (2 * pieces,), (pieces,), (3, 2), (3,), (2,), (1,),
        (layers,), (3,), (pieces // 2,),
    ]
    both = [
        ((turns, 2, *panel), bf16), ((turns, *panel), bf16),
        ((2 * pieces, *panel), bf16), ((pieces, *panel), bf16),
        ((pieces // 2, *panel), bf16),
    ]
    return [
        pltpu.VMEM((turns, 2, *panel), f32),
    ] + [
        pltpu.VMEM(*buffer) for buffer in both for _ in range(2)
    ] + [
        pltpu.VMEM((3, 2, *part), f32),
        pltpu.VMEM((3, 2, *part), bf16),
        pltpu.VMEM((3, *part), bf16),
        pltpu.VMEM((3, *part), bf16),
        pltpu.VMEM((2, *part), bf16),
        pltpu.VMEM((2, *part), bf16),
        pltpu.VMEM(part, bf16),
        pltpu.VMEM(part, bf16),
        pltpu.VMEM((LANES, layers, depth, width), bf16),
    ] + [pltpu.SemaphoreType.DMA(shape) for shape in sems for _ in range(2)]


def layered_kernel(
    cycle, pieces, back_pieces, features, behind, across, dense,
    weight_self, weight_neighbor, bias, cotangent,
    activations, grad_out, weight_self_out, weight_neighbor_out, bias_out,
    sent_t, grad_store, aggregate_store, grads,
    slots, blocks, total, rep_out, rep_in, first_sem, block_sem, *rest,
):
    sems, back = rest[:12], rest[12:]
    f32, bf16 = jnp.float32, jnp.bfloat16
    steps, rows = blocks.shape[0], blocks.shape[1]
    halves, half = total.shape[0], total.shape[2]
    size = rows // pieces
    at = Spot(cycle, steps)
    lane = at.lane
    diagonal = (1 - at.pair) * 2 + 1 - at.core
    layer_sems, pair_sems, core_sems, relay_sems, rep_sems, far_sems = [
        (sems[2 * k], sems[2 * k + 1]) for k in range(6)
    ]
    by_pair = pieces // 4
    partner = {"rep": 1 - at.replica}
    onward = {"blk": at.at_layer(at.sign)}

    def first(h, k):
        source, place = (
            (features, (0, lane)), (behind, (1, lane)), (across, (0, at.lane_across))
        )[k]
        return pltpu.make_async_copy(
            source.at[:, h * half : (h + 1) * half], slots.at[(*place, h)],
            first_sem.at[h, k],
        )

    for h in range(halves):
        for k in range(3):
            first(h, k).start()

    def load(step):
        return pltpu.make_async_copy(
            dense.at[step], blocks.at[step], block_sem.at[step]
        )

    @pl.loop(0, steps)
    def _(hop):
        load((steps - 1 - hop) * at.replica + hop * (1 - at.replica)).start()

    at.greet()
    for h in range(halves):
        for k in range(3):
            first(h, k).wait()

    def span(piece):
        return pl.ds(pl.multiple_of(piece * size, size), size)

    def layer_copy(h, d, p):
        return remote(slots.at[d, lane, h, span(p)], slots.at[d + 1, lane, h, span(p)],
                      layer_sems, (h, d, p), onward)

    def spot_copy(which, h, d, p):
        whose = at.lane_across if which == "relay" else lane
        here = slots.at[d, whose, h, span(p)]
        pack = {"pair": pair_sems, "core": core_sems, "relay": relay_sems}[which]
        device = at.across if which == "pair" else at.beside
        return remote(here, here, pack, (h, d, p), {"blk": device})

    def rep_copy(h, p):
        return remote(rep_out.at[h, span(p)], rep_in.at[h, span(p)], rep_sems, (h, p),
                      partner)

    def far_copy(h, p):
        whose = at.lane_across
        return remote(slots.at[1, whose, h, span(p)], slots.at[2, whose, h, span(p)],
                      far_sems, (h, p), onward)

    def sends_layer(p):
        return jnp.logical_or(
            at.chip_meets(at.pair, lane, 2),
            jnp.logical_and(p < by_pair, at.layer_meets(lane, 2)),
        )

    def sends_far(p):
        return jnp.logical_and(p >= by_pair, gets["pair"](2))

    def over_pair(d, p, kind):
        holds = kind["pair"](d)
        return jnp.logical_and(p < by_pair, holds) if d == 2 else holds

    sends = {
        "pair": lambda d: at.chip_meets(1 - at.pair, lane, d),
        "core": lambda d: at.meets(at.lane_beside, lane, d),
        "relay": lambda d: at.meets(at.lane_beside, at.lane_across, d),
    }
    gets = {
        "pair": lambda d: at.chip_meets(at.pair, at.lane_across, d),
        "core": lambda d: at.meets(lane, at.lane_beside, d),
        "relay": lambda d: at.meets(lane, diagonal, d),
    }

    def give(h, d, p, kinds):
        if "layer" in kinds:
            pl.when(sends_layer(p))(lambda: layer_copy(h, d, p).start())
        if "pair" in kinds:
            pl.when(over_pair(d, p, sends))(
                lambda: spot_copy("pair", h, d, p).start()
            )
        if "core" in kinds:
            pl.when(sends["core"](d))(lambda: spot_copy("core", h, d, p).start())

    def give_all(h, d, kinds):
        @pl.loop(0, pieces)
        def _(p):
            give(h, d, p, kinds)

    def arrive(h):
        @pl.loop(0, pieces)
        def _(p):
            @pl.when(sends_layer(p))
            def _():
                layer_copy(h, 1, p).wait_recv()
                give(h, 2, p, ("pair", "core"))

    def relay(h, d, then=None):
        @pl.loop(0, pieces)
        def _(p):
            @pl.when(gets["pair"](d))
            def _():
                if d > 0:
                    pl.when(over_pair(d, p, gets))(
                        lambda: spot_copy("pair", h, d, p).wait_recv()
                    )
                if d == 1:
                    pl.when(sends_far(p))(lambda: far_copy(h, p).start())
                if d == 2:
                    pl.when(sends_far(p))(lambda: far_copy(h, p).wait_recv())
                pl.when(sends["relay"](d))(
                    lambda: spot_copy("relay", h, d, p).start()
                )

            if then is not None:
                then(p)

    def gathered(h, d):
        for which in ("core", "relay"):
            @pl.when(gets[which](d))
            def _():
                @pl.loop(0, pieces)
                def _(p):
                    spot_copy(which, h, d, p).wait_recv()

    def multiply(h, d, place):
        @pl.loop(0, LANES)
        def _(source):
            step = at.step(lane, source, d)

            @pl.when(at.meets(lane, source, d))
            def _():
                total[h, place, :] += jnp.dot(
                    blocks[step, place, :], slots[d, source, h],
                    preferred_element_type=f32,
                )

    def await_blocks(d):
        @pl.loop(0, LANES)
        def _(source):
            @pl.when(at.meets(lane, source, d))
            def _():
                load(at.step(lane, source, d)).wait()

    def whole(h, d):
        gathered(h, d)
        if h == 0:
            await_blocks(d)
        multiply(h, d, slice(None))

    def last(h):
        gathered(h, 2)
        if h == 0:
            await_blocks(2)

        @pl.loop(0, pieces)
        def _(p):
            multiply(h, 2, span(p))
            rep_out[h, span(p)] = total[h, span(p)].astype(bf16)
            rep_copy(h, p).start()

    give_all(0, 1, ("layer", "pair", "core"))
    for h in range(halves):
        give_all(h, 0, ("core",))
        relay(h, 0)
    total[...] = jnp.zeros_like(total)
    whole(0, 0)
    relay(0, 1, lambda p: give(1, 1, p, ("pair", "core")))
    give_all(1, 1, ("layer",))
    arrive(0)
    whole(0, 1)
    relay(1, 1)
    relay(0, 2)
    last(0)
    arrive(1)
    whole(1, 0)
    whole(1, 1)
    relay(1, 2)
    last(1)

    def joined(ref, place):
        return jnp.concatenate([ref[h, place] for h in range(halves)], axis=1)

    def own_rows(place):
        return jnp.concatenate([slots[0, lane, h, place] for h in range(halves)], axis=1)

    @pl.loop(0, pieces)
    def _(p):
        place = span(p)
        for h in range(halves):
            rep_copy(h, p).wait_recv()
        mine, other = joined(rep_out, place), joined(rep_in, place)
        aggregate = (mine.astype(f32) + other.astype(f32)).astype(bf16)
        aggregate_store[place, :] = aggregate
        pre = (
            jnp.dot(own_rows(place), weight_self[...], preferred_element_type=f32)
            + jnp.dot(aggregate, weight_neighbor[...], preferred_element_type=f32)
            + bias[...]
        )
        sigmoid = jax.nn.sigmoid(pre)
        activations[place, :] = (pre * sigmoid).astype(activations.dtype)
        derivative = sigmoid * (1.0 + pre * (1.0 - sigmoid))
        grad_pre = (cotangent[place, :].astype(f32) * derivative).astype(bf16)
        grad_store[place, :] = grad_pre
        sent_t[:, place] = lax.dot_general(
            weight_neighbor[...], grad_pre, COLS_COLS, preferred_element_type=f32
        ).astype(sent_t.dtype)

    width = halves * half
    parts = grads.shape[0]
    depth = 2 * width // parts

    def fill_grads():
        grad_pre = grad_store[...]
        summed = jnp.sum(grad_pre.astype(f32), axis=0, keepdims=True)
        bias_rows = jnp.broadcast_to(
            summed, (grads.shape[1] - depth, width)
        ).astype(grads.dtype)
        for k in range(2):
            value = lax.dot_general(
                own_rows(slice(None)) if k == 0 else aggregate_store[...],
                grad_pre, ROWS_ROWS, preferred_element_type=f32,
            ).astype(grads.dtype)
            for part in range(parts // 2):
                rows_of = slice(part * depth, (part + 1) * depth)
                grads[k * (parts // 2) + part, 0:depth, :] = value[rows_of]
                grads[k * (parts // 2) + part, depth:, :] = bias_rows

    backward_part(
        cycle, back_pieces, weight_self, sent_t, grad_store, blocks, grads, fill_grads,
        grad_out, weight_self_out, weight_neighbor_out, bias_out, *back,
    )

    @pl.loop(0, pieces)
    def _(p):
        for h in range(halves):
            for d in range(3):
                if d == 1:
                    pl.when(sends_layer(p))(lambda: layer_copy(h, d, p).wait_send())
                    pl.when(sends_far(p))(lambda: far_copy(h, p).wait_send())
                if d > 0:
                    pl.when(over_pair(d, p, sends))(
                        lambda: spot_copy("pair", h, d, p).wait_send()
                    )
                for which in ("core", "relay"):
                    pl.when(sends[which](d))(
                        lambda: spot_copy(which, h, d, p).wait_send()
                    )
            rep_copy(h, p).wait_send()


def ahead_of_build(cycle, features):
    layers, places = cycle // LANES, [(g, r) for g in range(cycle) for r in range(2)]
    behind, across = [], []
    for group, replica in places:
        sign = 1 - 2 * replica
        layer, lane = group // LANES, group % LANES
        target = (layer + sign) % layers * LANES + lane
        behind.append((group * 2 + replica, target * 2 + replica))
        if lane // 2 == replica:
            target = layer * LANES + (lane + 2) % LANES
            across.append((group * 2 + replica, target * 2 + replica))
    return [lax.ppermute(features, ("blk", "rep"), pairs) for pairs in (behind, across)]


def layered(
    cycle, features, behind, across, dense, weight_self, weight_neighbor, bias, cotangent
):
    step_count, row_total, _ = dense.shape
    width = features.shape[1]
    pieces, back_pieces, halves = 4, 4, 2
    half = width // halves
    part = (2 * width // cycle + 16, width)
    bf16, f32 = jnp.bfloat16, jnp.float32
    shape = jax.ShapeDtypeStruct
    vmem, anywhere = [
        pl.BlockSpec(memory_space=space) for space in (pltpu.VMEM, pl.ANY)
    ]
    sems = [(halves, 3, pieces)] * 4 + [(halves, pieces)] * 2
    return pl.pallas_call(
        functools.partial(layered_kernel, cycle, pieces, back_pieces),
        in_specs=[anywhere] * 4 + [vmem] * 4,
        out_specs=[vmem] * 5,
        out_shape=(
            shape((row_total, width), bf16),
            shape((row_total, width), bf16),
            shape((width, width), f32),
            shape((width, width), f32),
            shape((1, width), f32),
        ),
        scratch_shapes=[
            pltpu.VMEM((width, row_total), bf16),
            pltpu.VMEM((row_total, width), bf16),
            pltpu.VMEM((row_total, width), bf16),
            pltpu.VMEM((cycle, *part), bf16),
            pltpu.VMEM((3, LANES, halves, row_total, half), bf16),
            pltpu.VMEM(dense.shape, bf16),
            pltpu.VMEM((halves, row_total, half), f32),
            pltpu.VMEM((halves, row_total, half), bf16),
            pltpu.VMEM((halves, row_total, half), bf16),
            pltpu.SemaphoreType.DMA((halves, 3)),
            pltpu.SemaphoreType.DMA((step_count,)),
        ]
        + [pltpu.SemaphoreType.DMA(size) for size in sems for _ in range(2)]
        + backward_scratch(cycle, back_pieces, row_total, width, part),
        compiler_params=pltpu.CompilerParams(
            collective_id=3, has_side_effects=True, vmem_limit_bytes=47 * 2**20
        ),
        name="layered",
    )(features, behind, across, dense, weight_self, weight_neighbor, bias, cotangent)


def close_kernel(*refs):
    count = len(refs) // 2
    for source, target in zip(refs[:count], refs[count:]):
        target[...] = source[...]


def close(arrays):
    return pl.pallas_call(
        close_kernel,
        out_shape=tuple(jax.ShapeDtypeStruct(a.shape, a.dtype) for a in arrays),
        compiler_params=pltpu.CompilerParams(vmem_limit_bytes=8 * 2**20),
        name="close",
    )(*arrays)


def on_device(
    features,
    weight_self,
    weight_neighbor,
    bias_vector,
    tile_row,
    tile_column,
    tile_value,
    tile_count,
    tile_table,
    cotangent,
):
    f32, bf16 = jnp.float32, jnp.bfloat16
    cycle_length = lax.axis_size("blk")
    replicas = lax.axis_size("rep")
    step_count = cycle_length // replicas
    replica = lax.axis_index("rep")
    row_total, width = features.shape

    jump = jnp.minimum(replica, replicas - 1 - replica)
    jump_bits = max(replicas // 2 - 1, 0).bit_length()
    reverse = (2 * replica) // replicas

    def shifted(array, sign):
        for bit in range(jump_bits):
            by = sign * (step_count << bit)
            moved = jnp.where(
                reverse == 0,
                lax.ppermute(
                    array, "blk",
                    [(i, (i + by) % cycle_length) for i in range(cycle_length)],
                ),
                lax.ppermute(
                    array, "blk",
                    [(i, (i - by) % cycle_length) for i in range(cycle_length)],
                ),
            )
            array = jnp.where(jump // (1 << bit) % 2 == 1, moved, array)
        return array

    if is_layered(cycle_length, replicas):
        early = ahead_of_build(cycle_length, features)
    dense = build_dense(
        tile_row[0], tile_column[0], tile_value[0], tile_count[0], tile_table, row_total
    )
    if is_layered(cycle_length, replicas):
        results = close(layered(
            cycle_length, features, *early, dense, weight_self, weight_neighbor,
            bias_vector.reshape(1, width), cotangent,
        ))
        return (*results[:4], results[4][0])
    mine = forward(cycle_length, replicas, shifted(features, 1), dense)
    bit = 1
    while True:
        other = lax.ppermute(mine, "rep", [(i, i ^ bit) for i in range(replicas)])
        bit *= 2
        if bit >= replicas:
            break
        mine = (mine.astype(f32) + other.astype(f32)).astype(bf16)
    activations, sent_t, self_t, grads = layer(
        cycle_length, features, mine, other, weight_self, weight_neighbor,
        bias_vector.reshape(1, width), cotangent,
    )
    pushed, part = backward(cycle_length, replicas, sent_t, dense, grads)
    pushed, part = shifted(pushed, -1), shifted(part, -1)

    def over_replicas(array):
        bit = 1
        while 2 * bit < replicas:
            other = lax.ppermute(array, "rep", [(i, i ^ bit) for i in range(replicas)])
            array = (array.astype(f32) + other.astype(f32)).astype(bf16)
            bit *= 2
        return array

    weights, bias_rows, grad_t = finish(
        cycle_length, replicas, over_replicas(pushed), over_replicas(part), self_t
    )
    weights = weights.reshape(2 * width, width)
    grad_features = grad_t.T
    return (
        activations,
        grad_features,
        weights[:width],
        weights[width:],
        bias_rows[0],
    )


def solution(mesh):
    placed = (
        P("blk", None),
        P(),
        P(),
        P(),
        P("blk", "rep", None),
        P("blk", "rep", None),
        P("blk", "rep", None),
        P("blk", "rep"),
        P(("blk", "rep"), None, None),
        P("blk", None),
    )
    return jax.shard_map(
        on_device,
        mesh=mesh,
        in_specs=placed,
        out_specs=(P("blk", None), P("blk", None), P(), P(), P()),
        check_vma=False,
    )
```

```python
import functools

import jax
import jax.numpy as jnp
from jax import lax
from jax.experimental import pallas as pl
from jax.experimental.pallas import tpu as pltpu
from jax.sharding import PartitionSpec as P

ROWS_ROWS = (((0,), (0,)), ((), ()))
COLS_COLS = (((1,), (1,)), ((), ()))


def build_kernel(rows, columns, values, counts, table, dense):
    step = pl.program_id(0)
    tile = table.shape[1]
    dense[...] = jnp.zeros_like(dense)

    def add_tile(slot, carry):
        row = pl.multiple_of(rows[step, slot] * tile, tile)
        column = pl.multiple_of(columns[step, slot] * tile, tile)
        place = (0, pl.ds(row, tile), pl.ds(column, tile))
        dense[place] = dense[place] + table[values[step, slot]]
        return carry

    lax.fori_loop(0, counts[step], add_tile, 0)


def build_dense(rows, columns, values, counts, table, row_total):
    step_count = rows.shape[0]
    return pl.pallas_call(
        build_kernel,
        grid_spec=pltpu.PrefetchScalarGridSpec(
            num_scalar_prefetch=4,
            grid=(step_count,),
            in_specs=[pl.BlockSpec(table.shape, lambda s, *_: (0, 0, 0))],
            out_specs=pl.BlockSpec((1, row_total, row_total), lambda s, *_: (s, 0, 0)),
        ),
        out_shape=jax.ShapeDtypeStruct((step_count, row_total, row_total), jnp.bfloat16),
        cost_estimate=pl.CostEstimate(
            flops=0, bytes_accessed=20 * 2**20, transcendentals=0
        ),
        name="build",
    )(rows, columns, values, counts, table)


def ring_place(cycle, replicas):
    group = lax.axis_index("blk")
    replica = lax.axis_index("rep")
    reverse = (2 * replica) // replicas if replicas > 1 else 0 * replica
    ahead = lax.rem(group + 1 - 2 * reverse + cycle, cycle)
    behind = lax.rem(group - 1 + 2 * reverse + cycle, cycle)
    return group, replica, reverse, ahead, behind


def greet(devices):
    barrier = pltpu.get_barrier_semaphore()
    for device in devices:
        pl.semaphore_signal(
            barrier, inc=1, device_id={"blk": device},
            device_id_type=pl.DeviceIdType.MESH,
        )
    pl.semaphore_wait(barrier, len(devices))


def forward_kernel(
    cycle, replicas, pieces, features, dense, out,
    slots, blocks, total, block_sem, first_sem, send_sem, recv_sem,
):
    steps, rows = blocks.shape[0], blocks.shape[1]
    _, _, reverse, ahead, behind = ring_place(cycle, replicas)
    size = rows // pieces
    first = pltpu.make_async_copy(features, slots.at[0], first_sem)
    first.start()

    def load(step):
        return pltpu.make_async_copy(
            dense.at[step], blocks.at[step], block_sem.at[step]
        )

    def in_order(hop):
        return hop * (1 - reverse) + (steps - hop) * reverse

    @pl.loop(0, steps)
    def _(hop):
        load(in_order(hop + reverse)).start()

    greet((ahead, behind))
    first.wait()

    def hop_copy(hop, piece):
        span = pl.ds(piece * size, size)
        return pltpu.make_async_remote_copy(
            src_ref=slots.at[hop, span],
            dst_ref=slots.at[hop + 1, span],
            send_sem=send_sem.at[hop, piece],
            recv_sem=recv_sem.at[hop, piece],
            device_id={"blk": ahead},
            device_id_type=pl.DeviceIdType.MESH,
        )

    total[...] = jnp.zeros_like(total)
    hops = steps - 1 + reverse

    @pl.loop(0, hops + 1)
    def _(hop):
        for piece in range(pieces):
            @pl.when(hop > 0)
            def _():
                hop_copy(hop - 1, piece).wait_recv()

            @pl.when(hop < hops)
            def _():
                hop_copy(hop, piece).start()

        step = in_order(hop)

        @pl.when(step < steps)
        def _():
            load(step).wait()
            total[...] += jnp.dot(
                blocks[step], slots[hop], preferred_element_type=jnp.float32
            )

    out[...] = total[...].astype(out.dtype)

    @pl.loop(0, hops)
    def _(hop):
        for piece in range(pieces):
            hop_copy(hop, piece).wait_send()


LANES = 4


def is_layered(cycle, replicas):
    return (
        cycle // replicas == 2 * LANES and cycle >= 3 * LANES
        and cycle % LANES == 0 and replicas == 2
    )


def forward(cycle, replicas, features, dense):
    step_count, row_total, _ = dense.shape
    width = features.shape[1]
    pieces = 4
    slots, sems = (step_count + 1, row_total, width), (step_count, pieces)
    return pl.pallas_call(
        functools.partial(forward_kernel, cycle, replicas, pieces),
        in_specs=[pl.BlockSpec(memory_space=pl.ANY)] * 2,
        out_specs=pl.BlockSpec(memory_space=pltpu.VMEM),
        out_shape=jax.ShapeDtypeStruct((row_total, width), jnp.bfloat16),
        scratch_shapes=[
            pltpu.VMEM(slots, jnp.bfloat16),
            pltpu.VMEM(dense.shape, jnp.bfloat16),
            pltpu.VMEM((row_total, width), jnp.float32),
            pltpu.SemaphoreType.DMA((step_count,)),
            pltpu.SemaphoreType.DMA,
            pltpu.SemaphoreType.DMA(sems),
            pltpu.SemaphoreType.DMA(sems),
        ],
        compiler_params=pltpu.CompilerParams(collective_id=0, has_side_effects=True),
        name="forward",
    )(features, dense)


def layer_kernel(
    features, mine, other, weight_self, weight_neighbor, bias, cotangent,
    activations, sent_t, self_t, grads,
):
    f32 = jnp.float32
    width = features.shape[1]
    aggregate = (mine[...].astype(f32) + other[...].astype(f32)).astype(jnp.bfloat16)
    pre = (
        jnp.dot(features[...], weight_self[...], preferred_element_type=f32)
        + jnp.dot(aggregate, weight_neighbor[...], preferred_element_type=f32)
        + bias[...]
    )
    sigmoid = jax.nn.sigmoid(pre)
    activations[...] = (pre * sigmoid).astype(activations.dtype)
    derivative = sigmoid * (1.0 + pre * (1.0 - sigmoid))
    grad_pre = (cotangent[...].astype(f32) * derivative).astype(jnp.bfloat16)
    sent_t[...] = lax.dot_general(
        weight_neighbor[...], grad_pre, COLS_COLS, preferred_element_type=f32
    ).astype(sent_t.dtype)
    self_t[...] = lax.dot_general(
        weight_self[...], grad_pre, COLS_COLS, preferred_element_type=f32
    )
    grad_self = lax.dot_general(
        features[...], grad_pre, ROWS_ROWS, preferred_element_type=f32
    ).astype(grads.dtype)
    grad_neighbor = lax.dot_general(
        aggregate, grad_pre, ROWS_ROWS, preferred_element_type=f32
    ).astype(grads.dtype)
    summed = jnp.sum(grad_pre.astype(f32), axis=0, keepdims=True)
    parts = grads.shape[0]
    depth = 2 * width // parts
    tail = grads.shape[1] - depth
    bias_rows = jnp.broadcast_to(summed, (tail, width)).astype(grads.dtype)
    for part in range(parts):
        source, place = (
            (grad_self, part) if 2 * part < parts else (grad_neighbor, part - parts // 2)
        )
        grads[part, 0:depth, :] = source[place * depth : (place + 1) * depth, :]
        grads[part, depth:, :] = bias_rows


def layer(parts, features, mine, other, weight_self, weight_neighbor, bias, cotangent):
    row_total, width = features.shape
    shape = jax.ShapeDtypeStruct
    return pl.pallas_call(
        layer_kernel,
        out_shape=(
            shape((row_total, width), jnp.bfloat16),
            shape((width, row_total), jnp.bfloat16),
            shape((width, row_total), jnp.float32),
            shape((parts, 2 * width // parts + 16, width), jnp.bfloat16),
        ),
        name="layer",
    )(features, mine, other, weight_self, weight_neighbor, bias, cotangent)


def backward_kernel(
    cycle, replicas, pieces, sent_t, dense, grads, out, part_out,
    landed, held, part_landed, part_held, blocks, term,
    block_sem, send_sem, recv_sem,
):
    steps = blocks.shape[0]
    width = sent_t.shape[0]
    size = width // pieces
    f32 = jnp.float32
    group, replica, reverse, behind, ahead = ring_place(cycle, replicas)

    def load(step):
        return pltpu.make_async_copy(
            dense.at[step], blocks.at[step], block_sem.at[step]
        )

    def in_order(hop):
        return (steps - 1 - hop) * (1 - reverse) + hop * reverse

    @pl.loop(0, steps)
    def _(hop):
        load(in_order(hop)).start()

    greet((ahead, behind))

    def hop_copy(hop, piece):
        if piece < pieces:
            span = pl.ds(piece * size, size)
            source, target = held.at[hop, span], landed.at[hop, span]
        else:
            source, target = part_held.at[hop], part_landed.at[hop]
        return pltpu.make_async_remote_copy(
            src_ref=source,
            dst_ref=target,
            send_sem=send_sem.at[hop, piece],
            recv_sem=recv_sem.at[hop, piece],
            device_id={"blk": ahead},
            device_id_type=pl.DeviceIdType.MESH,
        )

    hops = steps - 1 + reverse

    @pl.loop(0, steps)
    def _(hop):
        step = in_order(hop)
        target = lax.rem(group - steps * replica - step + 2 * cycle, cycle)
        load(step).wait()
        term[...] = jnp.dot(sent_t[...], blocks[step], preferred_element_type=f32)
        for piece in range(pieces + 1):
            span = pl.ds(piece * size, size)

            @pl.when(hop > 0)
            def _():
                hop_copy(hop - 1, piece).wait_recv()
                if piece < pieces:
                    held[hop, span] = (
                        term[span] + landed[hop - 1, span].astype(f32)
                    ).astype(held.dtype)
                else:
                    part_held[hop] = (
                        grads[target].astype(f32) + part_landed[hop - 1].astype(f32)
                    ).astype(part_held.dtype)

            @pl.when(hop == 0)
            def _():
                if piece < pieces:
                    held[hop, span] = term[span].astype(held.dtype)
                else:
                    part_held[hop] = grads[target]

            @pl.when(hop < hops)
            def _():
                hop_copy(hop, piece).start()

    @pl.when(reverse == 0)
    def _():
        out[...] = held[steps - 1]
        part_out[...] = part_held[steps - 1]

    @pl.when(reverse == 1)
    def _():
        for piece in range(pieces + 1):
            hop_copy(steps - 1, piece).wait_recv()
        out[...] = landed[steps - 1]
        part_out[...] = part_landed[steps - 1]

    @pl.loop(0, hops)
    def _(hop):
        for piece in range(pieces + 1):
            hop_copy(hop, piece).wait_send()


def backward(cycle, replicas, sent_t, dense, grads):
    step_count, row_total, _ = dense.shape
    width = sent_t.shape[0]
    part = grads.shape[1:]
    pieces = 4
    bf16 = jnp.bfloat16
    return pl.pallas_call(
        functools.partial(backward_kernel, cycle, replicas, pieces),
        in_specs=[
            pl.BlockSpec(memory_space=pltpu.VMEM),
            pl.BlockSpec(memory_space=pl.ANY),
            pl.BlockSpec(memory_space=pltpu.VMEM),
        ],
        out_specs=[pl.BlockSpec(memory_space=pltpu.VMEM)] * 2,
        out_shape=(
            jax.ShapeDtypeStruct((width, row_total), bf16),
            jax.ShapeDtypeStruct(part, bf16),
        ),
        scratch_shapes=[
            pltpu.VMEM((step_count, width, row_total), bf16),
            pltpu.VMEM((step_count, width, row_total), bf16),
            pltpu.VMEM((step_count, *part), bf16),
            pltpu.VMEM((step_count, *part), bf16),
            pltpu.VMEM(dense.shape, bf16),
            pltpu.VMEM((width, row_total), jnp.float32),
            pltpu.SemaphoreType.DMA((step_count,)),
            pltpu.SemaphoreType.DMA((step_count, pieces + 1)),
            pltpu.SemaphoreType.DMA((step_count, pieces + 1)),
        ],
        compiler_params=pltpu.CompilerParams(collective_id=1, has_side_effects=True),
        name="backward",
    )(sent_t, dense, grads)


def finish_kernel(
    cycle, replicas, pushed, part, self_t, weights, bias_out, grad_t,
    gathered, landed, part_landed, pair_send, pair_recv, send_sem, recv_sem,
):
    f32 = jnp.float32
    depth = gathered.shape[1]
    group = lax.axis_index("blk")
    partner = {"rep": lax.rem(lax.axis_index("rep") + replicas // 2, replicas)}
    mesh_id = pl.DeviceIdType.MESH
    barrier = pltpu.get_barrier_semaphore()
    pl.semaphore_signal(barrier, inc=1, device_id=partner, device_id_type=mesh_id)
    for away in range(1, cycle):
        pl.semaphore_signal(
            barrier, inc=1, device_id={"blk": lax.rem(group + away, cycle)},
            device_id_type=mesh_id,
        )
    pl.semaphore_wait(barrier, cycle)

    def swap(source, target, index):
        return pltpu.make_async_remote_copy(
            src_ref=source, dst_ref=target,
            send_sem=pair_send.at[index], recv_sem=pair_recv.at[index],
            device_id=partner, device_id_type=mesh_id,
        )

    part_swap = swap(part, part_landed, 0)
    part_swap.start()
    panel_swap = swap(pushed, landed, 1)
    panel_swap.start()
    part_swap.wait()
    summed = part[...].astype(f32) + part_landed[...].astype(f32)
    bias_out[...] = summed[depth:]
    gathered[group] = summed[:depth].astype(gathered.dtype)

    def put(away):
        return pltpu.make_async_remote_copy(
            src_ref=gathered.at[group],
            dst_ref=gathered.at[group],
            send_sem=send_sem.at[away],
            recv_sem=recv_sem.at[away],
            device_id={"blk": lax.rem(group + away, cycle)},
            device_id_type=mesh_id,
        )

    @pl.loop(1, cycle)
    def _(away):
        put(away).start()

    @pl.loop(1, cycle)
    def _(away):
        put(away).wait()

    weights[...] = gathered[...].astype(f32)
    panel_swap.wait()
    grad_t[...] = (
        self_t[...] + (pushed[...].astype(f32) + landed[...].astype(f32))
    ).astype(grad_t.dtype)


def finish(cycle, replicas, pushed, part, self_t):
    width = pushed.shape[0]
    depth = 2 * width // cycle
    tail = part.shape[0] - depth
    shape = jax.ShapeDtypeStruct
    return pl.pallas_call(
        functools.partial(finish_kernel, cycle, replicas),
        in_specs=[pl.BlockSpec(memory_space=pltpu.VMEM)] * 3,
        out_specs=[pl.BlockSpec(memory_space=pltpu.VMEM)] * 3,
        out_shape=(
            shape((cycle, depth, width), jnp.float32),
            shape((tail, width), jnp.float32),
            shape(pushed.shape, jnp.bfloat16),
        ),
        scratch_shapes=[
            pltpu.VMEM((cycle, depth, width), jnp.bfloat16),
            pltpu.VMEM(pushed.shape, jnp.bfloat16),
            pltpu.VMEM(part.shape, jnp.bfloat16),
            pltpu.SemaphoreType.DMA((2,)),
            pltpu.SemaphoreType.DMA((2,)),
            pltpu.SemaphoreType.DMA((cycle,)),
            pltpu.SemaphoreType.DMA((cycle,)),
        ],
        compiler_params=pltpu.CompilerParams(collective_id=2, has_side_effects=True),
        name="finish",
    )(pushed, part, self_t)


class Spot:
    def __init__(self, cycle, steps):
        self.steps, self.layers = steps, cycle // LANES
        self.group, self.replica = lax.axis_index("blk"), lax.axis_index("rep")
        self.sign = 1 - 2 * self.replica
        self.layer, self.lane = self.group // LANES, lax.rem(self.group, LANES)
        self.pair, self.core = self.lane // 2, lax.rem(self.lane, 2)
        self.lane_across = (1 - self.pair) * 2 + self.core
        self.lane_beside = self.pair * 2 + 1 - self.core
        self.across = self.layer * LANES + self.lane_across
        self.beside = self.layer * LANES + self.lane_beside

    def layer_at(self, distance):
        return lax.rem(self.layer + distance + 2 * self.layers, self.layers)

    def at_layer(self, distance):
        return self.layer_at(distance) * LANES + self.lane

    def step(self, lane, other_lane, distance):
        return (
            self.replica * self.steps + lane - other_lane
            + self.sign * LANES * distance
        )

    def meets(self, lane, other_lane, distance):
        step = self.step(lane, other_lane, distance)
        return jnp.logical_and(step >= 0, step < self.steps)

    def chip_meets(self, pair, other_lane, distance):
        return jnp.logical_or(
            self.meets(2 * pair, other_lane, distance),
            self.meets(2 * pair + 1, other_lane, distance),
        )

    def layer_meets(self, other_lane, distance):
        return jnp.logical_or(
            self.chip_meets(0, other_lane, distance),
            self.chip_meets(1, other_lane, distance),
        )

    def greet(self):
        barrier = pltpu.get_barrier_semaphore()
        signal = functools.partial(
            pl.semaphore_signal, barrier, inc=1, device_id_type=pl.DeviceIdType.MESH
        )
        signal(device_id={"blk": self.across})
        signal(device_id={"blk": self.beside})
        signal(device_id={"rep": 1 - self.replica})
        for away in range(1, self.layers):
            signal(device_id={"blk": self.at_layer(away)})
        pl.semaphore_wait(barrier, 2 + self.layers)


def remote(source, target, sems, index, device):
    send, recv = sems
    return pltpu.make_async_remote_copy(
        src_ref=source, dst_ref=target,
        send_sem=send.at[index], recv_sem=recv.at[index],
        device_id=device, device_id_type=pl.DeviceIdType.MESH,
    )


def backward_part(
    cycle, pieces, weight_self, sent_t, grad_pre, blocks, grads, fill_grads,
    grad_out, weight_self_out, weight_neighbor_out, bias_out,
    acc, core_out, core_in, pair_out, pair_in, layer_out, layer_in,
    rep_out, rep_in, far_out, far_in, part_acc, core_part, pair_part_out, pair_part,
    layer_part_out, layer_part, rep_part_out, rep_part, gathered, *sems,
):
    f32 = jnp.float32
    bf16 = jnp.bfloat16
    steps, rows = blocks.shape[0], blocks.shape[1]
    size = rows // pieces
    at = Spot(cycle, steps)
    layers = at.layers
    depth = gathered.shape[2]
    (core_sems, pair_sems, layer_sems, rep_sems, core_part_sems, pair_part_sems,
     layer_part_sems, rep_part_sems, spread_sems, widen_sems, far_sems) = [
        (sems[2 * k], sems[2 * k + 1]) for k in range(11)
    ]
    by_layer = pieces // 4
    group = pieces // 2
    partner = {"rep": 1 - at.replica}
    onward = {"blk": at.at_layer(-at.sign)}

    def own_lane(side):
        return 2 * side + at.core

    def other_lane(side):
        return 2 * side + 1 - at.core

    def span(n):
        return pl.ds(pl.multiple_of(n * size, size), size)

    def core_copy(i, side):
        return remote(core_out.at[i, side], core_in.at[i, side], core_sems, (i, side),
                      {"blk": at.beside})

    def pair_copy(i):
        return remote(pair_out.at[i], pair_in.at[i], pair_sems, i, {"blk": at.across})

    def layer_copy(i):
        return remote(layer_out.at[i], layer_in.at[i], layer_sems, i, onward)

    def far_copy(n):
        return remote(far_out.at[n], far_in.at[n], far_sems, n, onward)

    def rep_copy(n):
        return remote(rep_out.at[n], rep_in.at[n], rep_sems, n, partner)

    def part_of(d, lane):
        return at.layer_at(-at.sign * d) * LANES + lane

    def core_part_copy(d, side):
        return remote(grads.at[part_of(d, other_lane(side))], core_part.at[d, side],
                      core_part_sems, (d, side), {"blk": at.beside})

    def pair_part_copy(d):
        return remote(pair_part_out.at[d], pair_part.at[d], pair_part_sems, d,
                      {"blk": at.across})

    def layer_part_copy(d):
        return remote(layer_part_out.at[d - 1], layer_part.at[d - 1], layer_part_sems,
                      d - 1, onward)

    def rep_part_copy():
        return remote(rep_part_out, rep_part, rep_part_sems, 0, partner)

    def spread(away):
        here = gathered.at[at.lane, at.layer]
        return remote(here, here, spread_sems, away, {"blk": at.at_layer(away)})

    def widen(k):
        lane = at.lane_across if k == 2 else at.lane
        device = at.across if k == 0 else at.beside
        return remote(gathered.at[lane], gathered.at[lane], widen_sems, k,
                      {"blk": device})

    core_sends = [[at.meets(at.lane, other_lane(k), d) for k in range(2)] for d in range(3)]
    core_gets = [
        [at.meets(at.lane_beside, own_lane(k), d) for k in range(2)] for d in range(3)
    ]
    owns = [[at.meets(at.lane, own_lane(k), d) for k in range(2)] for d in range(3)]
    pair_sends = [at.chip_meets(at.pair, at.lane_across, d) for d in range(3)]
    pair_gets = [at.chip_meets(1 - at.pair, at.lane, d) for d in range(3)]
    chip_far = at.chip_meets(at.pair, at.lane, 2)
    layer_far = at.layer_meets(at.lane, 2)

    def sends_far(n):
        return jnp.logical_and(n < by_layer, pair_sends[2])

    def sends_core(d, side):
        return core_sends[d][side]

    def gets_core(d, side):
        return core_gets[d][side]

    def late(here, d, n):
        return here if d < 2 or n is None else jnp.logical_and(here, n >= by_layer)

    def sends_pair(d, n=None):
        return late(pair_sends[d], d, n)

    def gets_pair(d, n=None):
        return late(pair_gets[d], d, n)

    def sends_layer(d, n=None):
        if d < 2:
            return True
        if n is None:
            return layer_far
        return jnp.logical_or(chip_far, jnp.logical_and(layer_far, n >= by_layer))

    def when(condition):
        return (lambda act: act()) if condition is True else pl.when(condition)

    def product(i, d, n, lane, store):
        step = at.step(at.lane, lane, d)
        width = group * size
        wide = pl.ds(pl.multiple_of(n * size, width), width)
        value = jnp.dot(
            sent_t[...], blocks[step, :, wide], preferred_element_type=f32
        )
        for k in range(group):
            store(i + k, value[:, k * size : (k + 1) * size])

    def begin(d, n):
        i = (2 - d) * pieces + n
        for side in range(2):
            @pl.when(sends_core(d, side))
            def _():
                def store(i, value):
                    core_out[i, side] = value.astype(bf16)

                product(i, d, n, other_lane(side), store)
                for k in range(group):
                    core_copy(i + k, side).start()

        for side in range(2):
            own = owns[d][side]

            @pl.when(own)
            def _():
                def store(i, value):
                    acc[i, side] = value

                product(i, d, n, own_lane(side), store)

            @pl.when(jnp.logical_not(own))
            def _():
                for k in range(group):
                    acc[i + k, side] = jnp.zeros(acc.shape[2:], f32)

    def over_pair(d, n):
        i = (2 - d) * pieces + n
        for side in range(2):
            @pl.when(gets_core(d, side))
            def _():
                core_copy(i, side).wait_recv()
                acc[i, side] += core_in[i, side].astype(f32)

        if d > 0:
            @pl.when(sends_far(n))
            def _():
                if d == 2:
                    far_out[n] = acc[i, 1 - at.pair].astype(bf16)
                    far_copy(n).start()
                else:
                    far_copy(n).wait_recv()
                    acc[i, 1 - at.pair] += far_in[n].astype(f32)

        @pl.when(sends_pair(d, n))
        def _():
            pair_out[i] = acc[i, 1 - at.pair].astype(bf16)
            pair_copy(i).start()

    def over_layers(d, n):
        i = (2 - d) * pieces + n

        @pl.when(gets_pair(d, n))
        def _():
            pair_copy(i).wait_recv()
            acc[i, at.pair] += pair_in[i].astype(f32)

        if d < 2:
            @when(sends_layer(d + 1, n))
            def _():
                layer_copy(i - pieces).wait_recv()
                acc[i, at.pair] += layer_in[i - pieces].astype(f32)

        if d > 0:
            @when(sends_layer(d, n))
            def _():
                layer_out[i] = acc[i, at.pair].astype(bf16)
                layer_copy(i).start()
        else:
            rep_out[n] = acc[i, at.pair].astype(bf16)
            rep_copy(n).start()

            @pl.when(n > 0)
            def _():
                close(n - 1)

    def parts_to_core():
        fill_grads()
        for d in range(3):
            for side in range(2):
                pl.when(sends_core(d, side))(
                    lambda: core_part_copy(d, side).start()
                )

    def parts_to_pair():
        for d in range(3):
            for side in range(2):
                own = owns[d][side]
                part_acc[d, side] = grads[part_of(d, own_lane(side))].astype(
                    f32
                ) * own.astype(f32)

                @pl.when(gets_core(d, side))
                def _():
                    core_part_copy(d, side).wait_recv()
                    part_acc[d, side] += core_part[d, side].astype(f32)

            @pl.when(sends_pair(d))
            def _():
                pair_part_out[d] = part_acc[d, 1 - at.pair].astype(bf16)
                pair_part_copy(d).start()

    def part_onward(d):
        @pl.when(gets_pair(d))
        def _():
            pair_part_copy(d).wait_recv()
            part_acc[d, at.pair] += pair_part[d].astype(f32)

        if d < 2:
            @when(sends_layer(d + 1))
            def _():
                layer_part_copy(d + 1).wait_recv()
                part_acc[d, at.pair] += layer_part[d].astype(f32)

        if d > 0:
            @when(sends_layer(d))
            def _():
                layer_part_out[d - 1] = part_acc[d, at.pair].astype(bf16)
                layer_part_copy(d).start()
        else:
            rep_part_out[...] = part_acc[0, at.pair].astype(bf16)
            rep_part_copy().start()

    def part_spread():
        rep_part_copy().wait_recv()
        summed = rep_part_out[...].astype(f32) + rep_part[...].astype(f32)
        bias_out[...] = summed[depth : depth + 1]
        gathered[at.lane, at.layer] = summed[:depth].astype(bf16)
        for away in range(1, layers):
            spread(away).start()

    def part_over_pair():
        for away in range(1, layers):
            spread(away).wait_recv()
        widen(0).start()

    def part_over_core():
        widen(0).wait_recv()
        widen(1).start()
        widen(2).start()

    def close(n):
        rep_copy(n).wait_recv()
        pushed = rep_out[n].astype(f32) + rep_in[n].astype(f32)
        own = lax.dot_general(
            grad_pre[span(n), :], weight_self[...], COLS_COLS, preferred_element_type=f32
        )
        grad_out[span(n), :] = (own + pushed.T).astype(grad_out.dtype)

    quarter = pieces // 4
    timetable = (
        (2 * quarter, parts_to_core),
        (pieces, parts_to_pair),
        (pieces + 2 * quarter, functools.partial(part_onward, 2)),
        (2 * pieces + quarter, functools.partial(part_onward, 1)),
        (2 * pieces + 3 * quarter, functools.partial(part_onward, 0)),
        (3 * pieces, part_spread),
        (3 * pieces + 2 * quarter, part_over_pair),
        (3 * pieces + 3 * quarter, part_over_core),
    )

    for d in (2, 1, 0, -1):
        if d < 2:
            over_pair(d + 1, pieces - 1)

        @pl.loop(0, pieces)
        def _(n):
            if d >= 0:
                pl.when(n > 0)(lambda: over_pair(d, n - 1))
            if d < 2:
                over_layers(d + 1, n)
            if d >= 0:
                pl.when(lax.rem(n, group) == 0)(lambda: begin(d, n))
            for turn, act in timetable:
                if turn // pieces == 2 - d:
                    pl.when(n == turn % pieces)(act)

    widen(1).wait_recv()
    widen(2).wait_recv()
    per_weight = cycle // 2
    for layer in range(layers):
        for lane in range(LANES):
            part = layer * LANES + lane
            out = weight_self_out if part < per_weight else weight_neighbor_out
            place = part % per_weight * depth
            out[place : place + depth, :] = gathered[lane, layer].astype(f32)
    close(pieces - 1)

    @pl.loop(0, pieces)
    def _(n):
        for d in range(3):
            i = (2 - d) * pieces + n
            for side in range(2):
                pl.when(sends_core(d, side))(lambda: core_copy(i, side).wait_send())
            pl.when(sends_pair(d, n))(lambda: pair_copy(i).wait_send())
            if d > 0:
                when(sends_layer(d, n))(lambda: layer_copy(i).wait_send())
        rep_copy(n).wait_send()
        pl.when(sends_far(n))(lambda: far_copy(n).wait_send())

    for d in range(3):
        for side in range(2):
            pl.when(sends_core(d, side))(lambda: core_part_copy(d, side).wait_send())
        pl.when(sends_pair(d))(lambda: pair_part_copy(d).wait_send())
        if d > 0:
            when(sends_layer(d))(lambda: layer_part_copy(d).wait_send())
    rep_part_copy().wait_send()
    for away in range(1, layers):
        spread(away).wait_send()
    for k in range(3):
        widen(k).wait_send()


def backward_scratch(cycle, pieces, row_total, width, part):
    depth = 2 * width // cycle
    panel = (width, row_total // pieces)
    bf16, f32 = jnp.bfloat16, jnp.float32
    layers = cycle // LANES
    turns = 3 * pieces
    sems = [
        (turns, 2), (turns,), (2 * pieces,), (pieces,), (3, 2), (3,), (2,), (1,),
        (layers,), (3,), (pieces // 2,),
    ]
    both = [
        ((turns, 2, *panel), bf16), ((turns, *panel), bf16),
        ((2 * pieces, *panel), bf16), ((pieces, *panel), bf16),
        ((pieces // 2, *panel), bf16),
    ]
    return [
        pltpu.VMEM((turns, 2, *panel), f32),
    ] + [
        pltpu.VMEM(*buffer) for buffer in both for _ in range(2)
    ] + [
        pltpu.VMEM((3, 2, *part), f32),
        pltpu.VMEM((3, 2, *part), bf16),
        pltpu.VMEM((3, *part), bf16),
        pltpu.VMEM((3, *part), bf16),
        pltpu.VMEM((2, *part), bf16),
        pltpu.VMEM((2, *part), bf16),
        pltpu.VMEM(part, bf16),
        pltpu.VMEM(part, bf16),
        pltpu.VMEM((LANES, layers, depth, width), bf16),
    ] + [pltpu.SemaphoreType.DMA(shape) for shape in sems for _ in range(2)]


def layered_kernel(
    cycle, pieces, back_pieces, features, behind, across, dense,
    weight_self, weight_neighbor, bias, cotangent,
    activations, grad_out, weight_self_out, weight_neighbor_out, bias_out,
    sent_t, grad_store, aggregate_store, grads,
    slots, blocks, total, rep_out, rep_in, first_sem, block_sem, *rest,
):
    sems, back = rest[:12], rest[12:]
    f32, bf16 = jnp.float32, jnp.bfloat16
    steps, rows = blocks.shape[0], blocks.shape[1]
    halves, half = total.shape[0], total.shape[2]
    size = rows // pieces
    at = Spot(cycle, steps)
    lane = at.lane
    diagonal = (1 - at.pair) * 2 + 1 - at.core
    layer_sems, pair_sems, core_sems, relay_sems, rep_sems, far_sems = [
        (sems[2 * k], sems[2 * k + 1]) for k in range(6)
    ]
    by_pair = pieces // 4
    partner = {"rep": 1 - at.replica}
    onward = {"blk": at.at_layer(at.sign)}

    def first(h, k):
        source, place = (
            (features, (0, lane)), (behind, (1, lane)), (across, (0, at.lane_across))
        )[k]
        return pltpu.make_async_copy(
            source.at[:, h * half : (h + 1) * half], slots.at[(*place, h)],
            first_sem.at[h, k],
        )

    for h in range(halves):
        for k in range(3):
            first(h, k).start()

    def load(step):
        return pltpu.make_async_copy(
            dense.at[step], blocks.at[step], block_sem.at[step]
        )

    @pl.loop(0, steps)
    def _(hop):
        load((steps - 1 - hop) * at.replica + hop * (1 - at.replica)).start()

    at.greet()
    for h in range(halves):
        for k in range(3):
            first(h, k).wait()

    def span(piece):
        return pl.ds(pl.multiple_of(piece * size, size), size)

    def layer_copy(h, d, p):
        return remote(slots.at[d, lane, h, span(p)], slots.at[d + 1, lane, h, span(p)],
                      layer_sems, (h, d, p), onward)

    def spot_copy(which, h, d, p):
        whose = at.lane_across if which == "relay" else lane
        here = slots.at[d, whose, h, span(p)]
        pack = {"pair": pair_sems, "core": core_sems, "relay": relay_sems}[which]
        device = at.across if which == "pair" else at.beside
        return remote(here, here, pack, (h, d, p), {"blk": device})

    def rep_copy(h, p):
        return remote(rep_out.at[h, span(p)], rep_in.at[h, span(p)], rep_sems, (h, p),
                      partner)

    def far_copy(h, p):
        whose = at.lane_across
        return remote(slots.at[1, whose, h, span(p)], slots.at[2, whose, h, span(p)],
                      far_sems, (h, p), onward)

    chip_far, layer_far = at.chip_meets(at.pair, lane, 2), at.layer_meets(lane, 2)

    def sends_layer(p):
        return jnp.logical_or(chip_far, jnp.logical_and(p < by_pair, layer_far))

    def sends_far(p):
        return jnp.logical_and(p >= by_pair, gets["pair"](2))

    def over_pair(d, p, kind):
        holds = kind["pair"](d)
        return jnp.logical_and(p < by_pair, holds) if d == 2 else holds

    def fixed(test):
        return [test(d) for d in range(3)].__getitem__

    sends = {
        "pair": fixed(lambda d: at.chip_meets(1 - at.pair, lane, d)),
        "core": fixed(lambda d: at.meets(at.lane_beside, lane, d)),
        "relay": fixed(lambda d: at.meets(at.lane_beside, at.lane_across, d)),
    }
    gets = {
        "pair": fixed(lambda d: at.chip_meets(at.pair, at.lane_across, d)),
        "core": fixed(lambda d: at.meets(lane, at.lane_beside, d)),
        "relay": fixed(lambda d: at.meets(lane, diagonal, d)),
    }

    def give(h, d, p, kinds):
        if "layer" in kinds:
            pl.when(sends_layer(p))(lambda: layer_copy(h, d, p).start())
        if "pair" in kinds:
            pl.when(over_pair(d, p, sends))(
                lambda: spot_copy("pair", h, d, p).start()
            )
        if "core" in kinds:
            pl.when(sends["core"](d))(lambda: spot_copy("core", h, d, p).start())

    def give_all(h, d, kinds):
        @pl.loop(0, pieces)
        def _(p):
            give(h, d, p, kinds)

    def arrive(h):
        @pl.loop(0, pieces)
        def _(p):
            @pl.when(sends_layer(p))
            def _():
                layer_copy(h, 1, p).wait_recv()
                give(h, 2, p, ("pair", "core"))

    def relay(h, d, then=None):
        @pl.loop(0, pieces)
        def _(p):
            @pl.when(gets["pair"](d))
            def _():
                if d > 0:
                    pl.when(over_pair(d, p, gets))(
                        lambda: spot_copy("pair", h, d, p).wait_recv()
                    )
                if d == 1:
                    pl.when(sends_far(p))(lambda: far_copy(h, p).start())
                if d == 2:
                    pl.when(sends_far(p))(lambda: far_copy(h, p).wait_recv())
                pl.when(sends["relay"](d))(
                    lambda: spot_copy("relay", h, d, p).start()
                )

            if then is not None:
                then(p)

    def gathered(h, d):
        for which in ("core", "relay"):
            @pl.when(gets[which](d))
            def _():
                @pl.loop(0, pieces)
                def _(p):
                    spot_copy(which, h, d, p).wait_recv()

    def multiply(h, d, place):
        @pl.loop(0, LANES)
        def _(source):
            step = at.step(lane, source, d)

            @pl.when(at.meets(lane, source, d))
            def _():
                total[h, place, :] += jnp.dot(
                    blocks[step, place, :], slots[d, source, h],
                    preferred_element_type=f32,
                )

    def await_blocks(d):
        @pl.loop(0, LANES)
        def _(source):
            @pl.when(at.meets(lane, source, d))
            def _():
                load(at.step(lane, source, d)).wait()

    def whole(h, d):
        gathered(h, d)
        if h == 0:
            await_blocks(d)
        multiply(h, d, slice(None))

    def last(h):
        gathered(h, 2)
        if h == 0:
            await_blocks(2)

        @pl.loop(0, pieces)
        def _(p):
            multiply(h, 2, span(p))
            rep_out[h, span(p)] = total[h, span(p)].astype(bf16)
            rep_copy(h, p).start()

    give_all(0, 1, ("layer", "pair", "core"))
    for h in range(halves):
        give_all(h, 0, ("core",))
        relay(h, 0)
    total[...] = jnp.zeros_like(total)
    whole(0, 0)
    relay(0, 1, lambda p: give(1, 1, p, ("pair", "core")))
    give_all(1, 1, ("layer",))
    arrive(0)
    whole(0, 1)
    relay(1, 1)
    whole(1, 0)
    relay(0, 2)
    last(0)
    arrive(1)
    whole(1, 1)
    relay(1, 2)
    last(1)

    def joined(ref, place):
        return jnp.concatenate([ref[h, place] for h in range(halves)], axis=1)

    def own_rows(place):
        return jnp.concatenate([slots[0, lane, h, place] for h in range(halves)], axis=1)

    @pl.loop(0, pieces)
    def _(p):
        place = span(p)
        for h in range(halves):
            rep_copy(h, p).wait_recv()
        mine, other = joined(rep_out, place), joined(rep_in, place)
        aggregate = (mine.astype(f32) + other.astype(f32)).astype(bf16)
        aggregate_store[place, :] = aggregate
        pre = (
            jnp.dot(own_rows(place), weight_self[...], preferred_element_type=f32)
            + jnp.dot(aggregate, weight_neighbor[...], preferred_element_type=f32)
            + bias[...]
        )
        sigmoid = jax.nn.sigmoid(pre)
        activations[place, :] = (pre * sigmoid).astype(activations.dtype)
        derivative = sigmoid * (1.0 + pre * (1.0 - sigmoid))
        grad_pre = (cotangent[place, :].astype(f32) * derivative).astype(bf16)
        grad_store[place, :] = grad_pre
        sent_t[:, place] = lax.dot_general(
            weight_neighbor[...], grad_pre, COLS_COLS, preferred_element_type=f32
        ).astype(sent_t.dtype)

    width = halves * half
    parts = grads.shape[0]
    depth = 2 * width // parts

    def fill_grads():
        grad_pre = grad_store[...]
        summed = jnp.sum(grad_pre.astype(f32), axis=0, keepdims=True)
        bias_rows = jnp.broadcast_to(
            summed, (grads.shape[1] - depth, width)
        ).astype(grads.dtype)
        for k in range(2):
            value = lax.dot_general(
                own_rows(slice(None)) if k == 0 else aggregate_store[...],
                grad_pre, ROWS_ROWS, preferred_element_type=f32,
            ).astype(grads.dtype)
            for part in range(parts // 2):
                rows_of = slice(part * depth, (part + 1) * depth)
                grads[k * (parts // 2) + part, 0:depth, :] = value[rows_of]
                grads[k * (parts // 2) + part, depth:, :] = bias_rows

    backward_part(
        cycle, back_pieces, weight_self, sent_t, grad_store, blocks, grads, fill_grads,
        grad_out, weight_self_out, weight_neighbor_out, bias_out, *back,
    )

    @pl.loop(0, pieces)
    def _(p):
        for h in range(halves):
            for d in range(3):
                if d == 1:
                    pl.when(sends_layer(p))(lambda: layer_copy(h, d, p).wait_send())
                    pl.when(sends_far(p))(lambda: far_copy(h, p).wait_send())
                if d > 0:
                    pl.when(over_pair(d, p, sends))(
                        lambda: spot_copy("pair", h, d, p).wait_send()
                    )
                for which in ("core", "relay"):
                    pl.when(sends[which](d))(
                        lambda: spot_copy(which, h, d, p).wait_send()
                    )
            rep_copy(h, p).wait_send()


def ahead_of_build(cycle, features):
    layers, places = cycle // LANES, [(g, r) for g in range(cycle) for r in range(2)]
    behind, across = [], []
    for group, replica in places:
        sign = 1 - 2 * replica
        layer, lane = group // LANES, group % LANES
        target = (layer + sign) % layers * LANES + lane
        behind.append((group * 2 + replica, target * 2 + replica))
        if lane // 2 == replica:
            target = layer * LANES + (lane + 2) % LANES
            across.append((group * 2 + replica, target * 2 + replica))
    return [lax.ppermute(features, ("blk", "rep"), pairs) for pairs in (behind, across)]


def layered(
    cycle, features, behind, across, dense, weight_self, weight_neighbor, bias, cotangent
):
    step_count, row_total, _ = dense.shape
    width = features.shape[1]
    pieces, back_pieces, halves = 4, 4, 2
    half = width // halves
    part = (2 * width // cycle + 16, width)
    bf16, f32 = jnp.bfloat16, jnp.float32
    shape = jax.ShapeDtypeStruct
    vmem, anywhere = [
        pl.BlockSpec(memory_space=space) for space in (pltpu.VMEM, pl.ANY)
    ]
    sems = [(halves, 3, pieces)] * 4 + [(halves, pieces)] * 2
    return pl.pallas_call(
        functools.partial(layered_kernel, cycle, pieces, back_pieces),
        in_specs=[anywhere] * 4 + [vmem] * 4,
        out_specs=[vmem] * 5,
        out_shape=(
            shape((row_total, width), bf16),
            shape((row_total, width), bf16),
            shape((width, width), f32),
            shape((width, width), f32),
            shape((1, width), f32),
        ),
        scratch_shapes=[
            pltpu.VMEM((width, row_total), bf16),
            pltpu.VMEM((row_total, width), bf16),
            pltpu.VMEM((row_total, width), bf16),
            pltpu.VMEM((cycle, *part), bf16),
            pltpu.VMEM((3, LANES, halves, row_total, half), bf16),
            pltpu.VMEM(dense.shape, bf16),
            pltpu.VMEM((halves, row_total, half), f32),
            pltpu.VMEM((halves, row_total, half), bf16),
            pltpu.VMEM((halves, row_total, half), bf16),
            pltpu.SemaphoreType.DMA((halves, 3)),
            pltpu.SemaphoreType.DMA((step_count,)),
        ]
        + [pltpu.SemaphoreType.DMA(size) for size in sems for _ in range(2)]
        + backward_scratch(cycle, back_pieces, row_total, width, part),
        compiler_params=pltpu.CompilerParams(
            collective_id=3, has_side_effects=True, vmem_limit_bytes=47 * 2**20
        ),
        name="layered",
    )(features, behind, across, dense, weight_self, weight_neighbor, bias, cotangent)


def close_kernel(*refs):
    count = len(refs) // 2
    for source, target in zip(refs[:count], refs[count:]):
        target[...] = source[...]


def close(arrays):
    return pl.pallas_call(
        close_kernel,
        out_shape=tuple(jax.ShapeDtypeStruct(a.shape, a.dtype) for a in arrays),
        compiler_params=pltpu.CompilerParams(vmem_limit_bytes=8 * 2**20),
        name="close",
    )(*arrays)


def on_device(
    features,
    weight_self,
    weight_neighbor,
    bias_vector,
    tile_row,
    tile_column,
    tile_value,
    tile_count,
    tile_table,
    cotangent,
):
    f32, bf16 = jnp.float32, jnp.bfloat16
    cycle_length = lax.axis_size("blk")
    replicas = lax.axis_size("rep")
    step_count = cycle_length // replicas
    replica = lax.axis_index("rep")
    row_total, width = features.shape

    jump = jnp.minimum(replica, replicas - 1 - replica)
    jump_bits = max(replicas // 2 - 1, 0).bit_length()
    reverse = (2 * replica) // replicas

    def shifted(array, sign):
        for bit in range(jump_bits):
            by = sign * (step_count << bit)
            moved = jnp.where(
                reverse == 0,
                lax.ppermute(
                    array, "blk",
                    [(i, (i + by) % cycle_length) for i in range(cycle_length)],
                ),
                lax.ppermute(
                    array, "blk",
                    [(i, (i - by) % cycle_length) for i in range(cycle_length)],
                ),
            )
            array = jnp.where(jump // (1 << bit) % 2 == 1, moved, array)
        return array

    if is_layered(cycle_length, replicas):
        early = ahead_of_build(cycle_length, features)
    dense = build_dense(
        tile_row[0], tile_column[0], tile_value[0], tile_count[0], tile_table, row_total
    )
    if is_layered(cycle_length, replicas):
        results = close(layered(
            cycle_length, features, *early, dense, weight_self, weight_neighbor,
            bias_vector.reshape(1, width), cotangent,
        ))
        return (*results[:4], results[4][0])
    mine = forward(cycle_length, replicas, shifted(features, 1), dense)
    bit = 1
    while True:
        other = lax.ppermute(mine, "rep", [(i, i ^ bit) for i in range(replicas)])
        bit *= 2
        if bit >= replicas:
            break
        mine = (mine.astype(f32) + other.astype(f32)).astype(bf16)
    activations, sent_t, self_t, grads = layer(
        cycle_length, features, mine, other, weight_self, weight_neighbor,
        bias_vector.reshape(1, width), cotangent,
    )
    pushed, part = backward(cycle_length, replicas, sent_t, dense, grads)
    pushed, part = shifted(pushed, -1), shifted(part, -1)

    def over_replicas(array):
        bit = 1
        while 2 * bit < replicas:
            other = lax.ppermute(array, "rep", [(i, i ^ bit) for i in range(replicas)])
            array = (array.astype(f32) + other.astype(f32)).astype(bf16)
            bit *= 2
        return array

    weights, bias_rows, grad_t = finish(
        cycle_length, replicas, over_replicas(pushed), over_replicas(part), self_t
    )
    weights = weights.reshape(2 * width, width)
    grad_features = grad_t.T
    return (
        activations,
        grad_features,
        weights[:width],
        weights[width:],
        bias_rows[0],
    )


def solution(mesh):
    placed = (
        P("blk", None),
        P(),
        P(),
        P(),
        P("blk", "rep", None),
        P("blk", "rep", None),
        P("blk", "rep", None),
        P("blk", "rep"),
        P(("blk", "rep"), None, None),
        P("blk", None),
    )
    return jax.shard_map(
        on_device,
        mesh=mesh,
        in_specs=placed,
        out_specs=(P("blk", None), P("blk", None), P(), P(), P()),
        check_vma=False,
    )
```
